32 devices in a mesh: dom: 16 (over z, y, x), spin: 2 (over core).
Axes of the slice: x: 2, y: 2, z: 4, core: 2. Of those that a mesh axis runs over, the one named last changes fastest.
Arguments:
- vectors: float32 [2, 8, 262144], P('spin', None, 'dom'), may hold values from -17 to 17
- basis: float32 [2, 16, 262144], P('spin', None, 'dom'), may hold values from -17 to 17
- potential: float32 [2, 262144], P('spin', 'dom'), may hold values from 1 to 3
- hop_table: bfloat16 [8, 128, 128], replicated, may hold values from -0.25 to 0.25
- soc_table: bfloat16 [2, 128, 128], replicated, may hold values from -0.5 to 0.5
- nbr_block: int32 [2048, 16], P('dom'), may hold values from 0 to 2047, as said below
- nbr_type: int32 [2048, 16], P('dom'), may hold values from 0 to 7
- nbr_count: int32 [2048], P('dom'), may hold values from 1 to 16, as said below
- flip_block: int32 [2048], P('dom'), may hold values from 0 to 2047, as said below
Outputs:
- block_one: float32 [2, 8, 262144], P('spin', None, 'dom')
- block_two: float32 [2, 8, 262144], P('spin', None, 'dom')
- coefs_one: float32 [32, 8], replicated
- coefs_two: float32 [40, 8], replicated
The draws below stay inside these ranges and needn't reach their ends.
Inputs may be any that keep to these rules, and one draw needn't show every extreme that they name: nbr_block[i, l] equals i + d modulo 2048 with -8 <= d <= 8; slots at or beyond nbr_count[i] are ignored; in slot 0, the first block of each group of 128 has d = -8 and the last has d = 8. `nbr_count`: some block has all 16 slots live. flip_block[i] lies in the same domain as i: flip_block[i] // 128 == i // 128.
All inputs are finite; a program needn't handle non-finite values.
Results may differ from the reference program's by a relative error of at most 0.0033.
Values may be sent and summed in bfloat16 or wider, within the bound.
A program may use at most 64 MiB of HBM per device.

```python
import math
import jax
import jax.numpy as jnp
from jax import lax

B = 128
K = 8
NB_DEV = 128
RANGE = 8
NTYPES = 8
MAXNB = 16
M = 16
NBLK = 2048
NORB = 262144


def orbital_scale(key, shape):
    spread = jax.random.uniform(key, shape, jnp.float32)
    return jnp.exp(spread * math.log(10.0)) / math.sqrt(99.0 / (2.0 * math.log(10.0)))


def draw_vectors(key, part):
    key_base, key_scale, key_column = jax.random.split(key, 3)
    base_values = jnp.clip(jax.random.normal(key_base, (2, K, NORB), jnp.float32), -6.0, 6.0)
    column_scale = jnp.exp(jax.random.uniform(key_column, (1, K, 1), jnp.float32, math.log(0.8), math.log(1.25)))
    return (base_values * column_scale * orbital_scale(key_scale, (2, 1, NORB))).astype(jnp.float32)


def draw_basis(key, part):
    key_base, key_scale, key_common = jax.random.split(key, 3)
    base_values = jnp.clip(jax.random.normal(key_base, (2, M, NORB), jnp.float32), -6.0, 6.0)
    shared_part = jnp.clip(jax.random.normal(key_common, (2, 1, NORB), jnp.float32), -6.0, 6.0)
    mixed_values = (base_values + 0.23 * shared_part) / math.sqrt(1.0529)
    return (mixed_values * orbital_scale(key_scale, (2, 1, NORB))).astype(jnp.float32)


def draw_nbr_block(key, part):
    block_rows = jnp.arange(NBLK, dtype=jnp.int32)[:, None]
    offset = jax.random.randint(key, (NBLK, MAXNB), -RANGE, RANGE + 1, dtype=jnp.int32)
    local_pos = block_rows % NB_DEV
    slot_zero = jnp.arange(MAXNB, dtype=jnp.int32)[None, :] == 0
    offset = jnp.where(slot_zero & (local_pos == 0), -RANGE, offset)
    offset = jnp.where(slot_zero & (local_pos == NB_DEV - 1), RANGE, offset)
    return ((block_rows + offset) % NBLK).astype(jnp.int32)


def draw_nbr_count(key, part):
    key_heavy, key_pick, key_row, key_count = jax.random.split(jax.random.fold_in(key, 17), 4)
    domain_total = NBLK // NB_DEV
    heavy_domain = jax.random.randint(key_heavy, (domain_total,), 0, 8, dtype=jnp.int32) == 0
    chosen_domain = jax.random.randint(key_pick, (), 0, domain_total, dtype=jnp.int32)
    heavy_domain = heavy_domain | (jnp.arange(domain_total, dtype=jnp.int32) == chosen_domain)
    slot_cap = jnp.where(heavy_domain, MAXNB, max(MAXNB // 4, 1)).astype(jnp.int32)
    cap_rows = jnp.repeat(slot_cap, NB_DEV)
    live_count = jax.random.randint(key_count, (NBLK,), 1, cap_rows + 1, dtype=jnp.int32)
    full_row = chosen_domain * NB_DEV + jax.random.randint(key_row, (), 0, NB_DEV, dtype=jnp.int32)
    live_count = jnp.where(jnp.arange(NBLK, dtype=jnp.int32) == full_row, MAXNB, live_count)
    return live_count.astype(jnp.int32)


def draw_flip_block(key, part):
    block_rows = jnp.arange(NBLK, dtype=jnp.int32)
    domain_start = block_rows // NB_DEV * NB_DEV
    return (domain_start + jax.random.randint(key, (NBLK,), 0, NB_DEV, dtype=jnp.int32)).astype(jnp.int32)


def with_ends(result, key, least, high):
    dims = result.shape
    spot = [jax.random.randint(jax.random.fold_in(key, axis), (), 0, dims[axis]) for axis in range(len(dims))]
    result = result.at[tuple(spot)].set(least)
    longest = dims.index(max(dims))
    spot[longest] = (spot[longest] + 1) % dims[longest]
    return result.at[tuple(spot)].set(high)


def block_scale(rng, dims, cuts, smallest, largest):
    loudness = 1.0
    for axis_at, shards_of in cuts:
        draws = jax.random.uniform(jax.random.fold_in(jax.random.fold_in(rng, 6), axis_at), (shards_of,), jnp.float32, smallest / len(cuts), largest / len(cuts))
        loudness = loudness * jnp.repeat(jnp.exp(draws), dims[axis_at] // shards_of).reshape((-1,) + (1,) * (len(dims) - 1 - axis_at))
    return loudness


def noise(rng, dims, scale, reach, kind=jnp.bfloat16):
    entries = jax.random.normal(rng, dims, jnp.float32) * scale
    return jnp.minimum(jnp.maximum(entries, -reach), reach).astype(kind)


def setup_inputs(seed: int = 0) -> dict:
    key_of = jax.random.split(jax.random.key(seed), 10)
    vectors = draw_vectors(jax.random.fold_in(key_of[9], 71), 0)
    basis = draw_basis(jax.random.fold_in(key_of[9], 71), 0)
    potential = jnp.clip(1.0 + 2.0 * jax.random.uniform(key_of[2], (2, NORB), jnp.float32) ** block_scale(key_of[2], (2, NORB), ((0, 2), (1, 16)), -0.2, 0.2), 1.0, 3.0)
    hop_table = noise(key_of[3], (NTYPES, B, B), (4 * B) ** -0.5, 0.25)
    soc_table = noise(key_of[4], (2, B, B), B ** -0.5, 0.5)
    nbr_block = draw_nbr_block(jax.random.fold_in(key_of[9], 71), 0)
    nbr_type = with_ends(jax.random.randint(key_of[6], (NBLK, MAXNB), 0, NTYPES), jax.random.fold_in(key_of[6], 1), 0, NTYPES - 1).astype(jnp.int32)
    nbr_count = draw_nbr_count(jax.random.fold_in(key_of[9], 71), 0)
    flip_block = draw_flip_block(jax.random.fold_in(key_of[9], 71), 0)
    return dict(vectors=vectors, basis=basis, potential=potential, hop_table=hop_table, soc_table=soc_table, nbr_block=nbr_block, nbr_type=nbr_type, nbr_count=nbr_count, flip_block=flip_block)


def hopping_image(rounded, hop_table, nbr_block, nbr_type, nbr_count):
    block_total = rounded.shape[2]
    domain_count = block_total // NB_DEV
    wrapped = jnp.concatenate([rounded[:, :, block_total - RANGE:], rounded, rounded[:, :, :RANGE]], axis=2)
    table_f32 = hop_table.astype(jnp.float32)
    local_index = jnp.arange(NB_DEV, dtype=jnp.int32)
    slot_index = jnp.arange(MAXNB, dtype=jnp.int32)

    def one_domain(domain):
        first_block = (domain * NB_DEV).astype(jnp.int32)
        extended = lax.dynamic_slice_in_dim(wrapped, first_block, NB_DEV + 2 * RANGE, 2).astype(jnp.float32)
        products = jnp.einsum('skjc,tbc->skjtb', extended, table_f32, precision=lax.Precision.HIGHEST)
        products = products.reshape(2, K, (NB_DEV + 2 * RANGE) * NTYPES, B)
        neighbours = lax.dynamic_slice_in_dim(nbr_block, first_block, NB_DEV, 0)
        types_here = lax.dynamic_slice_in_dim(nbr_type, first_block, NB_DEV, 0)
        counts_here = lax.dynamic_slice_in_dim(nbr_count, first_block, NB_DEV, 0)
        global_rows = first_block + local_index
        offset = (neighbours - global_rows[:, None] + RANGE) % block_total - RANGE
        flat_index = ((local_index[:, None] + RANGE + offset) * NTYPES + types_here).astype(jnp.int32)
        live_mask = (slot_index[None, :] < counts_here[:, None]).astype(jnp.float32)
        gathered = jnp.take(products, flat_index.reshape(-1), axis=2).reshape(2, K, NB_DEV, MAXNB, B)
        return jnp.sum(gathered * live_mask[None, None, :, :, None], axis=3)
    pieces = lax.map(one_domain, jnp.arange(domain_count, dtype=jnp.int32))
    return jnp.moveaxis(pieces, 0, 2).reshape(2, K, block_total, B)

def apply_operator(field, potential, hop_table, soc_table, nbr_block, nbr_type, nbr_count, flip_block):
    block_total = field.shape[2] // B
    rounded = field.reshape(2, K, block_total, B).astype(jnp.bfloat16)
    hopping = hopping_image(rounded, hop_table, nbr_block, nbr_type, nbr_count)
    other_side = jnp.take(rounded[::-1], flip_block, axis=2).astype(jnp.float32)
    flip_term = jnp.einsum('skic,sbc->skib', other_side, soc_table.astype(jnp.float32), precision=lax.Precision.HIGHEST)
    return potential[:, None, :] * field + (hopping + flip_term).reshape(2, K, -1)

def orthonormal(span, image):
    norm_count = float(2 * image.shape[2])
    highest = lax.Precision.HIGHEST
    first_coef = jnp.einsum('smn,skn->mk', span, image, precision=highest) / norm_count
    once = image - jnp.einsum('smn,mk->skn', span, first_coef, precision=highest)
    second_coef = jnp.einsum('smn,skn->mk', span, once, precision=highest) / norm_count
    twice = once - jnp.einsum('smn,mk->skn', span, second_coef, precision=highest)
    gram_matrix = jnp.einsum('skn,sln->kl', twice, twice, precision=highest) / norm_count
    lower_factor = jnp.linalg.cholesky(gram_matrix)
    rows_form = jnp.transpose(twice, (1, 0, 2)).reshape(K, -1)
    solved = lax.linalg.triangular_solve(lower_factor, rows_form, left_side=True, lower=True)
    new_block = jnp.transpose(solved.reshape(K, 2, -1), (1, 0, 2))
    coefs = jnp.concatenate([first_coef + second_coef, lower_factor.T], axis=0)
    return (new_block, coefs)

def reference(vectors, basis, potential, hop_table, soc_table, nbr_block, nbr_type, nbr_count, flip_block):
    image = apply_operator(vectors, potential, hop_table, soc_table, nbr_block, nbr_type, nbr_count, flip_block)
    span = jnp.concatenate([basis, vectors], axis=1)
    block_one, coefs_one = orthonormal(span, image)
    image_two = apply_operator(block_one, potential, hop_table, soc_table, nbr_block, nbr_type, nbr_count, flip_block)
    span_two = jnp.concatenate([span, block_one], axis=1)
    block_two, coefs_two = orthonormal(span_two, image_two)
    return (block_one, block_two, coefs_one, coefs_two)
```

```python
import functools
import jax
import jax.numpy as jnp
from jax import lax
from jax.experimental import pallas as pl
from jax.experimental.pallas import tpu as pltpu
from jax.sharding import PartitionSpec as P

RANGE = 8
STRIDE = 32
CHUNK = 16
MESH = pl.DeviceIdType.MESH
NT = (((1,), (1,)), ((), ()))
NN = (((1,), (0,)), ((), ()))
F32, BF16, I32 = jnp.float32, jnp.bfloat16, jnp.int32


def high_dot(left, right, dims):
    return lax.dot_general(
        left, right, dims, precision=lax.Precision.HIGHEST, preferred_element_type=F32
    )


def dot(left, right, dims):
    return lax.dot_general(left, right, dims, preferred_element_type=F32)


def split(value):
    low = value - value.astype(BF16).astype(F32)
    return jnp.concatenate([value, low], axis=0).astype(BF16)


def halves(value):
    high = value.astype(BF16)
    return high, (value - high.astype(F32)).astype(BF16)


def kernel(
    cfg,
    vec_hbm, basis_hbm, pot_hbm, hop_hbm, soc_hbm, nbr_hbm, type_hbm, count_hbm, flip_hbm,
    one_ref, split_ref, small_ref,
    vec_ref, basis_ref, pot_ref, hop_ref, soc_ref, nbr_ref, type_ref, count_ref, fliploc_ref,
    block_ref, edge_ref, major_ref, other_ref, near_ref, far_ref, prod_ref, edge_prod_ref,
    select_ref, edge_select_ref, fold_ref, stage_a_ref, stage_b_ref,
    load_sem, flip_send, flip_recv, edge_send, edge_recv, a_send, a_recv, b_send, b_recv,
):
    dom_total, group_doms, blocks, width, types, slots, vecs, kept, norm = cfg
    pair = 2 * vecs
    kept_groups = kept // vecs
    span_one = kept + vecs
    span_two = span_one + vecs
    rows_one = 2 * span_one
    rows_two = 2 * span_two
    count = blocks * width
    edge = RANGE * width
    kinds = (types + 1) * blocks

    sources = [
        (vec_hbm.at[0], vec_ref), (nbr_hbm, nbr_ref), (type_hbm, type_ref),
        (count_hbm, count_ref), (flip_hbm, fliploc_ref), (basis_hbm.at[0], basis_ref),
        (hop_hbm, hop_ref), (soc_hbm, soc_ref), (pot_hbm, pot_ref)]
    loads = [
        pltpu.make_async_copy(src, dst, load_sem.at[n]) for n, (src, dst) in enumerate(sources)]
    for copy in loads:
        copy.start()
    groups = dom_total // group_doms
    group_size = 2 * group_doms
    dom, spin = lax.axis_index("dom"), lax.axis_index("spin")
    rank_a = (dom % group_doms) * 2 + spin
    rank_b = dom // group_doms
    dom_base = rank_b * group_doms
    left, right = (dom + dom_total - 1) % dom_total, (dom + 1) % dom_total

    def peer_a(shift):
        other = (rank_a + shift) % group_size
        return (dom_base + other // 2, other % 2)

    def peer_b(shift):
        return (((rank_b + shift) % groups) * group_doms + dom % group_doms, spin)

    barrier = pltpu.get_barrier_semaphore()
    for shift in range(1, group_size):
        pl.semaphore_signal(barrier, inc=1, device_id=peer_a(shift), device_id_type=MESH)
    for shift in range(1, groups):
        pl.semaphore_signal(barrier, inc=1, device_id=peer_b(shift), device_id_type=MESH)
    for side in (left, right):
        pl.semaphore_signal(barrier, inc=1, device_id=(side, spin), device_id_type=MESH)

    lane = lax.broadcasted_iota(I32, (vecs, width), 1)
    row = lax.broadcasted_iota(I32, (vecs, width), 0)

    def cols(tile, size=1):
        return pl.ds(pl.multiple_of(tile * width, width), size * width)

    def flip_copy(app):
        return pltpu.make_async_remote_copy(
            src_ref=major_ref.at[app], dst_ref=other_ref.at[app],
            send_sem=flip_send.at[app], recv_sem=flip_recv.at[app],
            device_id=(dom, 1 - spin), device_id_type=MESH)

    def edge_copies(n, first, rows):
        part = pl.ds(first, rows)
        tail = pltpu.make_async_remote_copy(
            src_ref=split_ref.at[part, pl.ds(count - edge, edge)],
            dst_ref=edge_ref.at[part, pl.ds(0, edge)],
            send_sem=edge_send.at[n, 0], recv_sem=edge_recv.at[n, 0],
            device_id=(right, spin), device_id_type=MESH)
        head = pltpu.make_async_remote_copy(
            src_ref=split_ref.at[part, pl.ds(0, edge)],
            dst_ref=edge_ref.at[part, pl.ds(edge, edge)],
            send_sem=edge_send.at[n, 1], recv_sem=edge_recv.at[n, 1],
            device_id=(left, spin), device_id_type=MESH)
        return tail, head

    def to_major(value, scratch, base, store):
        for b in range(CHUNK):
            scratch[pl.ds(base + b * vecs, vecs), :] = value[:, b * width:(b + 1) * width]
        for k in range(vecs):
            store(k, scratch[pl.ds(base + k, CHUNK, stride=vecs), :].astype(BF16))

    def share(app, value):
        def stage(ref, send, recv, rank, size, peer, mine):
            ref[app, rank] = mine
            def copy(shift, slot):
                return pltpu.make_async_remote_copy(
                    src_ref=ref.at[app, rank], dst_ref=ref.at[app, slot],
                    send_sem=send.at[app, shift], recv_sem=recv.at[app, slot],
                    device_id=peer(shift), device_id_type=MESH)
            for shift in range(1, size):
                copy(shift, rank).start()
            for shift in range(1, size):
                copy(shift, (rank + size - shift) % size).wait_recv()
            for shift in range(1, size):
                copy(shift, rank).wait_send()
            total = ref[app, 0]
            for slot in range(1, size):
                total = total + ref[app, slot]
            return total
        value = stage(stage_a_ref, a_send, a_recv, rank_a, group_size, peer_a, value)
        if groups > 1:
            value = stage(stage_b_ref, b_send, b_recv, rank_b, groups, peer_b, value)
        return value * (1.0 / norm)

    def lanes(value, start, size):
        moved = value if start == 0 else pltpu.roll(value, width - start, 1)
        return jnp.where(lane < size, moved, 0.0)

    def tall(pieces):
        pad = width - vecs * len(pieces)
        return jnp.concatenate(list(pieces) + [jnp.zeros((pad, width), F32)], axis=0)

    def folded(value):
        wide = value.shape[1]
        fold_ref[:, pl.ds(0, wide)] = value[:vecs] + value[vecs:]
        both = fold_ref[...]
        both = both + pltpu.roll(both, width - vecs, 1)
        out = jnp.where(lane < vecs, both, 0.0)
        for g in range(1, wide // pair):
            inside = (lane >= vecs * g) & (lane < vecs * (g + 1))
            out = jnp.where(inside, pltpu.roll(both, width - vecs * g, 1), out)
        return out

    def gram(first, rows, size, start, stop):
        part = pl.ds(start * width, (stop - start) * width)
        return dot(split_ref[pl.ds(first, rows), part], split_ref[pl.ds(0, size), part], NT)

    def factor(first_t, image_gram, span_gram, span_count):
        total_t = 2.0 * first_t - high_dot(first_t, span_gram, NT)
        moved = high_dot(total_t, span_gram, NT) - first_t
        square = image_gram + high_dot(moved, tall([total_t]), NT) - high_dot(
            total_t, tall([first_t]), NT)
        table = jnp.where(lane < vecs, square, jnp.where(lane == row + vecs, 1.0, 0.0))
        table = table - pltpu.roll(total_t, pair, 1)
        lower = jnp.zeros((vecs, width), F32)
        for j in range(vecs):
            column = jnp.broadcast_to(table[:, j:j + 1], (vecs, width))
            pivot_row = jnp.broadcast_to(table[j:j + 1, :], (vecs, width))
            pivot = jnp.broadcast_to(column[j:j + 1, :], (vecs, width))
            scale = 1.0 / jnp.sqrt(pivot)
            lower = jnp.where((lane == j) & (row >= j), column * scale, lower)
            pivot_row = pivot_row * scale
            table = jnp.where(
                row == j, pivot_row, jnp.where(row > j, table - column * scale * pivot_row, table))
        mixer = jnp.zeros((vecs, width), F32)
        for g in range(span_count // vecs + 1):
            source = pair + vecs * g if g < span_count // vecs else vecs
            moved = pltpu.roll(table, (pair * g - source) % width, 1)
            mixer = jnp.where((lane >= pair * g) & (lane < pair * g + vecs), moved, mixer)
        mixer = mixer + pltpu.roll(mixer, vecs, 1)
        low = mixer - mixer.astype(BF16).astype(F32)
        return total_t + pltpu.roll(lower, span_count, 1), jnp.concatenate([mixer, low], axis=0)

    def products(app):
        source = major_ref[app].reshape(vecs * blocks, width)

        def body(two, carry):
            weights = hop_ref[pl.ds(pl.multiple_of(two * 2 * width, 2 * width), 2 * width), :]
            out = dot(source, weights, NT)
            for half in range(2):
                at = pl.multiple_of((two * 2 + half) * blocks, blocks)
                for k in range(vecs):
                    high, low = halves(
                        out[k * blocks:(k + 1) * blocks, half * width:(half + 1) * width])
                    side = pl.ds((k % 2) * width, width)
                    prod_ref[k // 2, pl.ds(at, blocks), side] = high
                    prod_ref[k // 2, pl.ds(kinds + at, blocks), side] = low
            return carry
        lax.fori_loop(0, types // 2, body, 0)

    def flip_products(app):
        out = dot(other_ref[app].reshape(vecs * blocks, width), soc_ref[spin], NT)
        for k in range(vecs):
            high, low = halves(out[k * blocks:(k + 1) * blocks])
            side = pl.ds((k % 2) * width, width)
            prod_ref[k // 2, pl.ds(types * blocks, blocks), side] = high
            prod_ref[k // 2, pl.ds(kinds + types * blocks, blocks), side] = low

    def gather():
        def body(two, carry):
            out = dot(select_ref[...], prod_ref[two], NN)
            for half in range(2):
                for i in range(blocks // vecs):
                    block_ref[pl.ds(i * vecs * vecs + 2 * two + half, vecs, stride=vecs), :] = (
                        out[i * vecs:(i + 1) * vecs, half * width:(half + 1) * width])
            return carry
        lax.fori_loop(0, vecs // 2, body, 0)

    def edge_gather():
        reach = 2 * RANGE
        source = far_ref[...].reshape(vecs * reach, width)

        def body(two, carry):
            weights = hop_ref[pl.ds(pl.multiple_of(two * 2 * width, 2 * width), 2 * width), :]
            out = dot(source, weights, NT)
            for half in range(2):
                at = pl.multiple_of((two * 2 + half) * reach, reach)
                for k in range(vecs):
                    high, low = halves(
                        out[k * reach:(k + 1) * reach, half * width:(half + 1) * width])
                    side = pl.ds((k % 2) * width, width)
                    edge_prod_ref[k // 2, pl.ds(at, reach), side] = high
                    edge_prod_ref[k // 2, pl.ds(types * reach + at, reach), side] = low
            return carry
        lax.fori_loop(0, types // 2, body, 0, unroll=True)
        for two in range(vecs // 2):
            out = dot(edge_select_ref[...], edge_prod_ref[two], NN)
            for half in range(2):
                for end, base in enumerate((0, (blocks - RANGE) * vecs)):
                    at = pl.ds(base + 2 * two + half, RANGE, stride=vecs)
                    block_ref[at, :] = block_ref[at, :] + out[
                        end * RANGE:(end + 1) * RANGE, half * width:(half + 1) * width]

    def assemble(field_ref, first, low, high):
        def body(block, carry):
            image = pot_ref[pl.ds(0, 1), cols(block)] * field_ref[:, cols(block)]
            at = pl.multiple_of(block * vecs, vecs)
            image = image + block_ref[pl.ds(at, vecs), :]
            split_ref[pl.ds(first, pair), cols(block)] = split(image)
            return carry
        lax.fori_loop(low, high, body, 0, unroll=8)

    def round_body(chunk, carry):
        value = vec_ref[:, cols(chunk * CHUNK, CHUNK)]
        split_ref[pl.ds(2 * kept, pair), cols(chunk * CHUNK, CHUNK)] = split(value)

        def store(k, rounded):
            major_ref[0, k, pl.ds(pl.multiple_of(chunk * CHUNK, CHUNK), CHUNK), :] = rounded
        to_major(value, block_ref, chunk * CHUNK * vecs, store)
        return carry

    def store_far(k, rounded):
        far_ref[k] = rounded

    chunks = blocks // CHUNK
    loads[0].wait()
    round_body(0, 0)
    round_body(chunks - 1, 0)
    pl.semaphore_wait(barrier, group_size - 1 + groups - 1 + 2)
    vec_edges = edge_copies(0, 2 * kept, pair)
    for copy in vec_edges:
        copy.start()
    lax.fori_loop(1, chunks - 1, round_body, 0)
    flip_one = flip_copy(0)
    flip_one.start()
    for copy in loads[1:6]:
        copy.wait()

    def split_basis(chunk, carry):
        part = cols(chunk * 4, 4)
        for g in range(kept_groups):
            split_ref[pl.ds(g * pair, pair), part] = split(basis_ref[pl.ds(g * vecs, vecs), part])
        return carry
    lax.fori_loop(0, blocks // 4, split_basis, 0, unroll=2)
    basis_edges = edge_copies(1, 0, 2 * kept)
    for copy in basis_edges:
        copy.start()

    local = lax.broadcasted_iota(I32, (slots, blocks), 1)
    slot_at = lax.broadcasted_iota(I32, (slots, blocks), 0)
    shift = nbr_ref[...] - (dom * blocks + local) + RANGE
    total = dom_total * blocks
    shift = jnp.where(shift < 0, shift + total, shift)
    shift = jnp.where(shift >= total, shift - total, shift)
    place = local + shift - RANGE
    live = slot_at < count_ref[...]
    inside = (place >= 0) & (place < blocks)
    code = jnp.where(live & inside, type_ref[...] * STRIDE + shift, -1)
    edge_code = jnp.where(place < 0, place + RANGE, place - blocks + RANGE)
    edge_code = jnp.where(live & ~inside, type_ref[...] * (2 * RANGE) + edge_code, -1)

    def counts(codes, base):
        wanted = row + base
        parts = [jnp.where(codes[s:s + 1, :] == wanted, 1.0, 0.0) for s in range(slots)]
        while len(parts) > 1:
            parts = [parts[p] + parts[p + 1] for p in range(0, len(parts), 2)]
        return parts[0]

    wide_row = lax.broadcasted_iota(I32, (width, width), 0)
    wide_lane = lax.broadcasted_iota(I32, (width, width), 1)
    band = (wide_lane - wide_row <= RANGE) & (wide_row - wide_lane <= RANGE)
    per_tile = width // STRIDE
    blank = jnp.zeros((vecs, width), F32)
    for tile in range(types // per_tile):
        pieces = []
        for r in range(width // vecs):
            live_rows = (r * vecs) % STRIDE <= 2 * RANGE
            pieces.append(counts(code, tile * width + r * vecs) if live_rows else blank)
        table = jnp.concatenate(pieces, axis=0).T
        for t in range(per_tile):
            moved = pltpu.roll(
                table, (-RANGE - STRIDE * t) % width, 1, stride=1, stride_axis=0)
            picked = jnp.where(band, moved, 0.0).astype(BF16)
            at = (tile * per_tile + t) * blocks
            select_ref[:, pl.ds(at, blocks)] = picked
            select_ref[:, pl.ds(kinds + at, blocks)] = picked
    flip_local = fliploc_ref[...] - dom * blocks
    picked = jnp.where(flip_local == wide_row, 1.0, 0.0).T.astype(BF16)
    select_ref[:, pl.ds(types * blocks, blocks)] = picked
    select_ref[:, pl.ds(kinds + types * blocks, blocks)] = picked
    table = jnp.concatenate(
        [counts(edge_code, r * vecs) for r in range(width // vecs)], axis=0).T
    picked = jnp.concatenate([table[:RANGE], table[blocks - RANGE:]], axis=0).astype(BF16)
    edge_select_ref[:, pl.ds(0, width)] = picked
    edge_select_ref[:, pl.ds(width, width)] = picked

    fold_ref[...] = jnp.zeros((vecs, width), F32)
    low_gram = gram(0, rows_one, rows_one, 0, blocks)
    packed_low = jnp.zeros((vecs, width), F32)
    for g in range(span_one // vecs):
        piece = folded(low_gram[g * pair:(g + 1) * pair])
        packed_low = packed_low + pltpu.roll(piece, span_two + g * span_one, 1)
    for copy in loads[6:]:
        copy.wait()

    products(0)
    flip_one.wait_recv()
    flip_products(0)
    gather()
    assemble(vec_ref, rows_one, RANGE, blocks - RANGE)
    result = gram(rows_one, pair, rows_two, RANGE, blocks - RANGE)
    for copy in vec_edges:
        copy.wait_recv()
    value = edge_ref[pl.ds(2 * kept, pair), :].astype(F32)[:vecs]
    to_major(value, near_ref, 0, store_far)
    edge_gather()
    assemble(vec_ref, rows_one, 0, RANGE)
    assemble(vec_ref, rows_one, blocks - RANGE, blocks)
    image_edges = edge_copies(2, rows_one, pair)
    for copy in image_edges:
        copy.start()
    result = result + gram(rows_one, pair, rows_two, 0, RANGE)
    result = result + gram(rows_one, pair, rows_two, blocks - RANGE, blocks)
    packed = share(0, folded(result) + packed_low)
    span_gram = tall(
        [lanes(packed, span_two + g * span_one, span_one) for g in range(span_one // vecs)])
    coefs, mixer = factor(
        lanes(packed, 0, span_one), lanes(packed, span_one, vecs), span_gram, span_one)
    small_ref[pl.ds(0, vecs), :] = coefs
    mixer = mixer.astype(BF16)[:, :rows_two]
    for copy in image_edges:
        copy.wait_send()
    for copy in image_edges + basis_edges:
        copy.wait_recv()

    def mix_body(chunk, carry):
        part = cols(chunk * CHUNK, CHUNK)
        out = dot(mixer, split_ref[pl.ds(0, rows_two), part], NN)
        value = out[:vecs] + out[vecs:]
        one_ref[:, part] = value
        split_ref[pl.ds(rows_one, pair), part] = split(value)

        def store(k, rounded):
            major_ref[1, k, pl.ds(pl.multiple_of(chunk * CHUNK, CHUNK), CHUNK), :] = rounded
        to_major(value, block_ref, chunk * CHUNK * vecs, store)
        return carry
    lax.fori_loop(0, chunks, mix_body, 0)
    flip_two = flip_copy(1)
    flip_two.start()
    products(1)
    out = dot(mixer, edge_ref[...], NN)
    to_major(out[:vecs] + out[vecs:], near_ref, 0, store_far)
    early = folded(gram(rows_one, pair, rows_two, 0, blocks))
    flip_two.wait_recv()
    flip_products(1)
    gather()
    edge_gather()
    assemble(one_ref, rows_two, 0, blocks)
    result = folded(gram(rows_two, pair, rows_two + pair, 0, blocks))
    packed = share(1, result + pltpu.roll(early, 64, 1))
    low = jnp.concatenate(
        [jnp.zeros((span_one, width), F32), lanes(packed, 64, span_two),
         jnp.zeros((width - span_two, width), F32)], axis=0)
    span_gram = span_gram + low + jnp.where(
        (wide_row < span_one) & (wide_lane >= span_one), low.T, 0.0)
    coefs, mixer = factor(
        lanes(packed, 0, span_two), lanes(packed, span_two, vecs), span_gram, span_two)
    small_ref[pl.ds(vecs, vecs), :] = coefs
    small_ref[pl.ds(pair, pair), :] = mixer
    for copy in vec_edges + basis_edges:
        copy.wait_send()
    flip_one.wait_send()
    flip_two.wait_send()


def finish(
    cfg, small_ref, split_ref, one_ref,
    one_hbm, two_hbm, coef_one_hbm, coef_two_hbm,
    two_ref, cut_one_ref, cut_two_ref, store_sem,
):
    _, _, blocks, width, _, _, vecs, kept, _ = cfg
    span_one = kept + vecs
    span_two = span_one + vecs
    pieces = 8
    size = blocks // pieces * width
    stores = [pltpu.make_async_copy(one_ref, one_hbm.at[0], store_sem.at[0])]
    stores[-1].start()
    mixer = small_ref[pl.ds(2 * vecs, 2 * vecs), :].astype(BF16)[:, :2 * (span_two + vecs)]
    for piece in range(pieces):
        part = pl.ds(piece * size, size)
        out = dot(mixer, split_ref[:, part], NN)
        two_ref[:, part] = out[:vecs] + out[vecs:]
        stores.append(pltpu.make_async_copy(
            two_ref.at[:, part], two_hbm.at[0, :, part], store_sem.at[1 + piece]))
        stores[-1].start()
    cut_one_ref[...] = small_ref[pl.ds(0, vecs), :span_one + vecs]
    cut_two_ref[...] = small_ref[pl.ds(vecs, vecs), :span_two + vecs]
    stores.append(pltpu.make_async_copy(cut_one_ref, coef_one_hbm, store_sem.at[1 + pieces]))
    stores.append(pltpu.make_async_copy(cut_two_ref, coef_two_hbm, store_sem.at[2 + pieces]))
    for copy in stores[-2:]:
        copy.start()
    for copy in stores:
        copy.wait()


def per_device(
    vectors, basis, potential, hop_table, soc_table, nbr_block, nbr_type, nbr_count, flip_block
):
    blocks, slots = nbr_block.shape
    types, width, _ = hop_table.shape
    vecs, kept = vectors.shape[1], basis.shape[1]
    dom_total = lax.axis_size("dom")
    group_doms = 4 if dom_total % 4 == 0 else 1
    groups = dom_total // group_doms
    norm = float(2 * blocks * width * dom_total)
    cfg = (dom_total, group_doms, blocks, width, types, slots, vecs, kept, norm)
    count = blocks * width
    pair = 2 * vecs
    span_one, span_two = kept + vecs, kept + 2 * vecs
    kinds = (types + 1) * blocks
    vmem = pl.BlockSpec(memory_space=pltpu.VMEM)
    hbm = pl.BlockSpec(memory_space=pltpu.HBM)
    dma = pltpu.SemaphoreType.DMA
    shape = jax.ShapeDtypeStruct
    one, parts, small = pl.pallas_call(
        functools.partial(kernel, cfg),
        name="krylov",
        out_shape=(
            pltpu.VMEM((vecs, count), F32),
            pltpu.VMEM((2 * (span_two + vecs), count), BF16),
            pltpu.VMEM((4 * vecs, width), F32),
        ),
        in_specs=[hbm] * 9,
        out_specs=(vmem, vmem, vmem),
        scratch_shapes=[
            pltpu.VMEM((vecs, count), F32),
            pltpu.VMEM((kept, count), F32),
            pltpu.VMEM((1, count), F32),
            pltpu.VMEM((types * width, width), BF16),
            pltpu.VMEM(soc_table.shape, BF16),
            pltpu.VMEM((slots, blocks), I32),
            pltpu.VMEM((slots, blocks), I32),
            pltpu.VMEM((1, blocks), I32),
            pltpu.VMEM((1, blocks), I32),
            pltpu.VMEM((blocks * vecs, width), F32),
            pltpu.VMEM((2 * span_two, 2 * RANGE * width), BF16),
            pltpu.VMEM((2, vecs, blocks, width), BF16),
            pltpu.VMEM((2, vecs, blocks, width), BF16),
            pltpu.VMEM((2 * RANGE * vecs, width), F32),
            pltpu.VMEM((vecs, 2 * RANGE, width), BF16),
            pltpu.VMEM((vecs // 2, 2 * kinds, 2 * width), BF16),
            pltpu.VMEM((vecs // 2, 4 * RANGE * types, 2 * width), BF16),
            pltpu.VMEM((blocks, 2 * kinds), BF16),
            pltpu.VMEM((2 * RANGE, 4 * RANGE * types), BF16),
            pltpu.VMEM((vecs, width), F32),
            pltpu.VMEM((2, 2 * group_doms, vecs, width), F32),
            pltpu.VMEM((2, groups, vecs, width), F32),
            dma((9,)),
            dma((2,)), dma((2,)),
            dma((3, 2)), dma((3, 2)),
            dma((2, 2 * group_doms)), dma((2, 2 * group_doms)),
            dma((2, groups)), dma((2, groups)),
        ],
        compiler_params=pltpu.CompilerParams(
            collective_id=0, has_side_effects=True, vmem_limit_bytes=32 * 1024 * 1024),
    )(
        vectors, basis, potential, hop_table.reshape(types * width, width), soc_table,
        nbr_block.T, nbr_type.T, nbr_count.reshape(1, blocks), flip_block.reshape(1, blocks))
    one, two, coef_one, coef_two = pl.pallas_call(
        functools.partial(finish, cfg),
        name="finish",
        out_shape=(
            shape((1, vecs, count), F32),
            shape((1, vecs, count), F32),
            shape((vecs, span_one + vecs), F32),
            shape((vecs, span_two + vecs), F32),
        ),
        in_specs=[vmem, vmem, vmem],
        out_specs=(hbm,) * 4,
        scratch_shapes=[
            pltpu.VMEM((vecs, count), F32),
            pltpu.VMEM((vecs, span_one + vecs), F32),
            pltpu.VMEM((vecs, span_two + vecs), F32),
            dma((11,)),
        ],
        compiler_params=pltpu.CompilerParams(vmem_limit_bytes=16 * 1024 * 1024),
    )(small, parts, one)
    return one, two, coef_one.T, coef_two.T


def solution(mesh):
    return jax.shard_map(
        per_device,
        mesh=mesh,
        in_specs=(
            P("spin", None, "dom"),
            P("spin", None, "dom"),
            P("spin", "dom"),
            P(),
            P(),
            P("dom", None),
            P("dom", None),
            P("dom"),
            P("dom"),
        ),
        out_specs=(P("spin", None, "dom"), P("spin", None, "dom"), P(), P()),
        check_vma=False,
    )
```

```python
import functools
import jax
import jax.numpy as jnp
from jax import lax
from jax.experimental import pallas as pl
from jax.experimental.pallas import tpu as pltpu
from jax.sharding import PartitionSpec as P

RANGE = 8
STRIDE = 32
CHUNK = 16
MESH = pl.DeviceIdType.MESH
NT = (((1,), (1,)), ((), ()))
NN = (((1,), (0,)), ((), ()))
F32, BF16, I32 = jnp.float32, jnp.bfloat16, jnp.int32


def high_dot(left, right, dims):
    return lax.dot_general(
        left, right, dims, precision=lax.Precision.HIGHEST, preferred_element_type=F32
    )


def dot(left, right, dims):
    return lax.dot_general(left, right, dims, preferred_element_type=F32)


def split(value):
    low = value - value.astype(BF16).astype(F32)
    return jnp.concatenate([value, low], axis=0).astype(BF16)


def halves(value):
    high = value.astype(BF16)
    return high, (value - high.astype(F32)).astype(BF16)


def kernel(
    cfg,
    vec_hbm, basis_hbm, pot_hbm, hop_hbm, soc_hbm, nbr_hbm, type_hbm, count_hbm, flip_hbm,
    one_ref, split_ref, small_ref,
    vec_ref, basis_ref, pot_ref, hop_ref, soc_ref, nbr_ref, type_ref, count_ref, fliploc_ref,
    block_ref, edge_ref, major_ref, other_ref, near_ref, far_ref, prod_ref, edge_prod_ref,
    select_ref, edge_select_ref, fold_ref, stage_a_ref, stage_b_ref,
    load_sem, flip_send, flip_recv, edge_send, edge_recv, a_send, a_recv, b_send, b_recv,
):
    dom_total, group_doms, blocks, width, types, slots, vecs, kept, norm = cfg
    pair = 2 * vecs
    kept_groups = kept // vecs
    span_one = kept + vecs
    span_two = span_one + vecs
    rows_one = 2 * span_one
    rows_two = 2 * span_two
    count = blocks * width
    edge = RANGE * width
    kinds = (types + 1) * blocks

    sources = [
        (vec_hbm.at[0], vec_ref), (nbr_hbm, nbr_ref), (type_hbm, type_ref),
        (count_hbm, count_ref), (flip_hbm, fliploc_ref), (basis_hbm.at[0], basis_ref),
        (hop_hbm, hop_ref), (soc_hbm, soc_ref), (pot_hbm, pot_ref)]
    loads = [
        pltpu.make_async_copy(src, dst, load_sem.at[n]) for n, (src, dst) in enumerate(sources)]
    for copy in loads:
        copy.start()
    groups = dom_total // group_doms
    group_size = 2 * group_doms
    dom, spin = lax.axis_index("dom"), lax.axis_index("spin")
    rank_a = (dom % group_doms) * 2 + spin
    rank_b = dom // group_doms
    dom_base = rank_b * group_doms
    left, right = (dom + dom_total - 1) % dom_total, (dom + 1) % dom_total

    def peer_a(shift):
        other = (rank_a + shift) % group_size
        return (dom_base + other // 2, other % 2)

    def peer_b(shift):
        return (((rank_b + shift) % groups) * group_doms + dom % group_doms, spin)

    barrier = pltpu.get_barrier_semaphore()
    for shift in range(1, group_size):
        pl.semaphore_signal(barrier, inc=1, device_id=peer_a(shift), device_id_type=MESH)
    for shift in range(1, groups):
        pl.semaphore_signal(barrier, inc=1, device_id=peer_b(shift), device_id_type=MESH)
    for side in (left, right):
        pl.semaphore_signal(barrier, inc=1, device_id=(side, spin), device_id_type=MESH)

    lane = lax.broadcasted_iota(I32, (vecs, width), 1)
    row = lax.broadcasted_iota(I32, (vecs, width), 0)

    def cols(tile, size=1):
        return pl.ds(pl.multiple_of(tile * width, width), size * width)

    def flip_copy(app):
        return pltpu.make_async_remote_copy(
            src_ref=major_ref.at[app], dst_ref=other_ref.at[app],
            send_sem=flip_send.at[app], recv_sem=flip_recv.at[app],
            device_id=(dom, 1 - spin), device_id_type=MESH)

    def edge_copies(n, first, rows):
        part = pl.ds(first, rows)
        tail = pltpu.make_async_remote_copy(
            src_ref=split_ref.at[part, pl.ds(count - edge, edge)],
            dst_ref=edge_ref.at[part, pl.ds(0, edge)],
            send_sem=edge_send.at[n, 0], recv_sem=edge_recv.at[n, 0],
            device_id=(right, spin), device_id_type=MESH)
        head = pltpu.make_async_remote_copy(
            src_ref=split_ref.at[part, pl.ds(0, edge)],
            dst_ref=edge_ref.at[part, pl.ds(edge, edge)],
            send_sem=edge_send.at[n, 1], recv_sem=edge_recv.at[n, 1],
            device_id=(left, spin), device_id_type=MESH)
        return tail, head

    def to_major(value, scratch, base, store):
        for b in range(CHUNK):
            scratch[pl.ds(base + b * vecs, vecs), :] = value[:, b * width:(b + 1) * width]
        for k in range(vecs):
            store(k, scratch[pl.ds(base + k, CHUNK, stride=vecs), :].astype(BF16))

    def share(app, value):
        def stage(ref, send, recv, rank, size, peer, mine):
            ref[app, rank] = mine
            def copy(shift, slot):
                return pltpu.make_async_remote_copy(
                    src_ref=ref.at[app, rank], dst_ref=ref.at[app, slot],
                    send_sem=send.at[app, shift], recv_sem=recv.at[app, slot],
                    device_id=peer(shift), device_id_type=MESH)
            for shift in range(1, size):
                copy(shift, rank).start()
            for shift in range(1, size):
                copy(shift, (rank + size - shift) % size).wait_recv()
            for shift in range(1, size):
                copy(shift, rank).wait_send()
            total = ref[app, 0]
            for slot in range(1, size):
                total = total + ref[app, slot]
            return total
        value = stage(stage_a_ref, a_send, a_recv, rank_a, group_size, peer_a, value)
        if groups > 1:
            value = stage(stage_b_ref, b_send, b_recv, rank_b, groups, peer_b, value)
        return value * (1.0 / norm)

    def lanes(value, start, size):
        moved = value if start == 0 else pltpu.roll(value, width - start, 1)
        return jnp.where(lane < size, moved, 0.0)

    def tall(pieces):
        pad = width - vecs * len(pieces)
        return jnp.concatenate(list(pieces) + [jnp.zeros((pad, width), F32)], axis=0)

    def folded(value):
        wide = value.shape[1]
        fold_ref[:, pl.ds(0, wide)] = value[:vecs] + value[vecs:]
        both = fold_ref[...]
        both = both + pltpu.roll(both, width - vecs, 1)
        out = jnp.where(lane < vecs, both, 0.0)
        for g in range(1, wide // pair):
            inside = (lane >= vecs * g) & (lane < vecs * (g + 1))
            out = jnp.where(inside, pltpu.roll(both, width - vecs * g, 1), out)
        return out

    def gram(first, rows, size, start, stop):
        part = pl.ds(start * width, (stop - start) * width)
        return dot(split_ref[pl.ds(first, rows), part], split_ref[pl.ds(0, size), part], NT)

    def factor(first_t, image_gram, span_gram, span_count):
        total_t = 2.0 * first_t - high_dot(first_t, span_gram, NT)
        moved = high_dot(total_t, span_gram, NT) - first_t
        square = image_gram + high_dot(moved, tall([total_t]), NT) - high_dot(
            total_t, tall([first_t]), NT)
        table = jnp.where(lane < vecs, square, jnp.where(lane == row + vecs, 1.0, 0.0))
        table = table - pltpu.roll(total_t, pair, 1)
        lower = jnp.zeros((vecs, width), F32)
        for j in range(vecs):
            column = jnp.broadcast_to(table[:, j:j + 1], (vecs, width))
            pivot_row = jnp.broadcast_to(table[j:j + 1, :], (vecs, width))
            pivot = jnp.broadcast_to(column[j:j + 1, :], (vecs, width))
            scale = 1.0 / jnp.sqrt(pivot)
            lower = jnp.where((lane == j) & (row >= j), column * scale, lower)
            pivot_row = pivot_row * scale
            table = jnp.where(
                row == j, pivot_row, jnp.where(row > j, table - column * scale * pivot_row, table))
        mixer = jnp.zeros((vecs, width), F32)
        for g in range(span_count // vecs + 1):
            source = pair + vecs * g if g < span_count // vecs else vecs
            moved = pltpu.roll(table, (pair * g - source) % width, 1)
            mixer = jnp.where((lane >= pair * g) & (lane < pair * g + vecs), moved, mixer)
        mixer = mixer + pltpu.roll(mixer, vecs, 1)
        low = mixer - mixer.astype(BF16).astype(F32)
        return total_t + pltpu.roll(lower, span_count, 1), jnp.concatenate([mixer, low], axis=0)

    def products(app):
        source = major_ref[app].reshape(vecs * blocks, width)

        def body(two, carry):
            weights = hop_ref[pl.ds(pl.multiple_of(two * 2 * width, 2 * width), 2 * width), :]
            out = dot(source, weights, NT)
            for half in range(2):
                at = pl.multiple_of((two * 2 + half) * blocks, blocks)
                for k in range(vecs):
                    high, low = halves(
                        out[k * blocks:(k + 1) * blocks, half * width:(half + 1) * width])
                    side = pl.ds((k % 2) * width, width)
                    prod_ref[k // 2, pl.ds(at, blocks), side] = high
                    prod_ref[k // 2, pl.ds(kinds + at, blocks), side] = low
            return carry
        lax.fori_loop(0, types // 2, body, 0)

    def flip_products(app):
        out = dot(other_ref[app].reshape(vecs * blocks, width), soc_ref[spin], NT)
        for k in range(vecs):
            high, low = halves(out[k * blocks:(k + 1) * blocks])
            side = pl.ds((k % 2) * width, width)
            prod_ref[k // 2, pl.ds(types * blocks, blocks), side] = high
            prod_ref[k // 2, pl.ds(kinds + types * blocks, blocks), side] = low

    def gather():
        def body(two, carry):
            out = dot(select_ref[...], prod_ref[two], NN)
            for half in range(2):
                for i in range(blocks // vecs):
                    block_ref[pl.ds(i * vecs * vecs + 2 * two + half, vecs, stride=vecs), :] = (
                        out[i * vecs:(i + 1) * vecs, half * width:(half + 1) * width])
            return carry
        lax.fori_loop(0, vecs // 2, body, 0)

    def edge_gather():
        reach = 2 * RANGE
        source = far_ref[...].reshape(vecs * reach, width)

        def body(two, carry):
            weights = hop_ref[pl.ds(pl.multiple_of(two * 2 * width, 2 * width), 2 * width), :]
            out = dot(source, weights, NT)
            for half in range(2):
                at = pl.multiple_of((two * 2 + half) * reach, reach)
                for k in range(vecs):
                    high, low = halves(
                        out[k * reach:(k + 1) * reach, half * width:(half + 1) * width])
                    side = pl.ds((k % 2) * width, width)
                    edge_prod_ref[k // 2, pl.ds(at, reach), side] = high
                    edge_prod_ref[k // 2, pl.ds(types * reach + at, reach), side] = low
            return carry
        lax.fori_loop(0, types // 2, body, 0, unroll=True)
        for two in range(vecs // 2):
            out = dot(edge_select_ref[...], edge_prod_ref[two], NN)
            for half in range(2):
                for end, base in enumerate((0, (blocks - RANGE) * vecs)):
                    at = pl.ds(base + 2 * two + half, RANGE, stride=vecs)
                    block_ref[at, :] = block_ref[at, :] + out[
                        end * RANGE:(end + 1) * RANGE, half * width:(half + 1) * width]

    def assemble(field_ref, first, low, high):
        def body(block, carry):
            image = pot_ref[pl.ds(0, 1), cols(block)] * field_ref[:, cols(block)]
            at = pl.multiple_of(block * vecs, vecs)
            image = image + block_ref[pl.ds(at, vecs), :]
            split_ref[pl.ds(first, pair), cols(block)] = split(image)
            return carry
        lax.fori_loop(low, high, body, 0, unroll=8)

    def round_body(chunk, carry):
        value = vec_ref[:, cols(chunk * CHUNK, CHUNK)]
        split_ref[pl.ds(2 * kept, pair), cols(chunk * CHUNK, CHUNK)] = split(value)

        def store(k, rounded):
            major_ref[0, k, pl.ds(pl.multiple_of(chunk * CHUNK, CHUNK), CHUNK), :] = rounded
        to_major(value, block_ref, chunk * CHUNK * vecs, store)
        return carry

    def store_far(k, rounded):
        far_ref[k] = rounded

    chunks = blocks // CHUNK
    loads[0].wait()
    round_body(0, 0)
    round_body(chunks - 1, 0)
    pl.semaphore_wait(barrier, group_size - 1 + groups - 1 + 2)
    vec_edges = edge_copies(0, 2 * kept, pair)
    for copy in vec_edges:
        copy.start()
    lax.fori_loop(1, chunks - 1, round_body, 0)
    flip_one = flip_copy(0)
    flip_one.start()
    for copy in loads[1:6]:
        copy.wait()

    def split_basis(chunk, carry):
        part = cols(chunk * 4, 4)
        for g in range(kept_groups):
            split_ref[pl.ds(g * pair, pair), part] = split(basis_ref[pl.ds(g * vecs, vecs), part])
        return carry
    lax.fori_loop(0, blocks // 4, split_basis, 0, unroll=2)
    basis_edges = edge_copies(1, 0, 2 * kept)
    for copy in basis_edges:
        copy.start()

    local = lax.broadcasted_iota(I32, (slots, blocks), 1)
    slot_at = lax.broadcasted_iota(I32, (slots, blocks), 0)
    shift = nbr_ref[...] - (dom * blocks + local) + RANGE
    total = dom_total * blocks
    shift = jnp.where(shift < 0, shift + total, shift)
    shift = jnp.where(shift >= total, shift - total, shift)
    place = local + shift - RANGE
    live = slot_at < count_ref[...]
    inside = (place >= 0) & (place < blocks)
    code = jnp.where(live & inside, type_ref[...] * STRIDE + shift, -1)
    edge_code = jnp.where(place < 0, place + RANGE, place - blocks + RANGE)
    edge_code = jnp.where(live & ~inside, type_ref[...] * (2 * RANGE) + edge_code, -1)

    def counts(codes, base):
        wanted = row + base
        parts = [jnp.where(codes[s:s + 1, :] == wanted, 1.0, 0.0) for s in range(slots)]
        while len(parts) > 1:
            parts = [parts[p] + parts[p + 1] for p in range(0, len(parts), 2)]
        return parts[0]

    wide_row = lax.broadcasted_iota(I32, (width, width), 0)
    wide_lane = lax.broadcasted_iota(I32, (width, width), 1)
    band = (wide_lane - wide_row <= RANGE) & (wide_row - wide_lane <= RANGE)
    per_tile = width // STRIDE
    blank = jnp.zeros((vecs, width), F32)
    for tile in range(types // per_tile):
        pieces = []
        for r in range(width // vecs):
            live_rows = (r * vecs) % STRIDE <= 2 * RANGE
            pieces.append(counts(code, tile * width + r * vecs) if live_rows else blank)
        table = jnp.concatenate(pieces, axis=0).T
        for t in range(per_tile):
            moved = pltpu.roll(
                table, (-RANGE - STRIDE * t) % width, 1, stride=1, stride_axis=0)
            picked = jnp.where(band, moved, 0.0).astype(BF16)
            at = (tile * per_tile + t) * blocks
            select_ref[:, pl.ds(at, blocks)] = picked
            select_ref[:, pl.ds(kinds + at, blocks)] = picked
    flip_local = fliploc_ref[...] - dom * blocks
    picked = jnp.where(flip_local == wide_row, 1.0, 0.0).T.astype(BF16)
    select_ref[:, pl.ds(types * blocks, blocks)] = picked
    select_ref[:, pl.ds(kinds + types * blocks, blocks)] = picked
    table = jnp.concatenate(
        [counts(edge_code, r * vecs) for r in range(width // vecs)], axis=0).T
    picked = jnp.concatenate([table[:RANGE], table[blocks - RANGE:]], axis=0).astype(BF16)
    edge_select_ref[:, pl.ds(0, width)] = picked
    edge_select_ref[:, pl.ds(width, width)] = picked

    fold_ref[...] = jnp.zeros((vecs, width), F32)
    low_gram = gram(0, rows_one, rows_one, 0, blocks)
    packed_low = jnp.zeros((vecs, width), F32)
    for g in range(span_one // vecs):
        piece = folded(low_gram[g * pair:(g + 1) * pair])
        packed_low = packed_low + pltpu.roll(piece, span_two + g * span_one, 1)
    for copy in loads[6:]:
        copy.wait()

    products(0)
    flip_one.wait_recv()
    flip_products(0)
    gather()
    assemble(vec_ref, rows_one, RANGE, blocks - RANGE)
    result = gram(rows_one, pair, rows_two, RANGE, blocks - RANGE)
    for copy in vec_edges:
        copy.wait_recv()
    value = edge_ref[pl.ds(2 * kept, pair), :].astype(F32)[:vecs]
    to_major(value, near_ref, 0, store_far)
    edge_gather()
    assemble(vec_ref, rows_one, 0, RANGE)
    assemble(vec_ref, rows_one, blocks - RANGE, blocks)
    image_edges = edge_copies(2, rows_one, pair)
    for copy in image_edges:
        copy.start()
    result = result + gram(rows_one, pair, rows_two, 0, RANGE)
    result = result + gram(rows_one, pair, rows_two, blocks - RANGE, blocks)
    packed = share(0, folded(result) + packed_low)
    span_gram = tall(
        [lanes(packed, span_two + g * span_one, span_one) for g in range(span_one // vecs)])
    coefs, mixer = factor(
        lanes(packed, 0, span_one), lanes(packed, span_one, vecs), span_gram, span_one)
    small_ref[pl.ds(0, vecs), :] = coefs
    mixer = mixer.astype(BF16)[:, :rows_two]
    for copy in image_edges:
        copy.wait_send()
    for copy in image_edges + basis_edges:
        copy.wait_recv()

    def mix_body(chunk, carry):
        part = cols(chunk * CHUNK, CHUNK)
        out = dot(mixer, split_ref[pl.ds(0, rows_two), part], NN)
        value = out[:vecs] + out[vecs:]
        one_ref[:, part] = value
        split_ref[pl.ds(rows_one, pair), part] = split(value)

        def store(k, rounded):
            major_ref[1, k, pl.ds(pl.multiple_of(chunk * CHUNK, CHUNK), CHUNK), :] = rounded
        to_major(value, block_ref, chunk * CHUNK * vecs, store)
        return carry
    lax.fori_loop(0, chunks, mix_body, 0)
    flip_two = flip_copy(1)
    flip_two.start()
    products(1)
    out = dot(mixer, edge_ref[...], NN)
    to_major(out[:vecs] + out[vecs:], near_ref, 0, store_far)
    early = folded(gram(rows_one, pair, rows_two, 0, blocks))
    flip_two.wait_recv()
    flip_products(1)
    gather()
    edge_gather()
    assemble(one_ref, rows_two, 0, blocks)
    result = folded(gram(rows_two, pair, rows_two + pair, 0, blocks))
    packed = share(1, result + pltpu.roll(early, 64, 1))
    low = jnp.concatenate(
        [jnp.zeros((span_one, width), F32), lanes(packed, 64, span_two),
         jnp.zeros((width - span_two, width), F32)], axis=0)
    span_gram = span_gram + low + jnp.where(
        (wide_row < span_one) & (wide_lane >= span_one), low.T, 0.0)
    coefs, mixer = factor(
        lanes(packed, 0, span_two), lanes(packed, span_two, vecs), span_gram, span_two)
    small_ref[pl.ds(vecs, vecs), :] = coefs
    small_ref[pl.ds(pair, pair), :] = mixer
    for copy in vec_edges + basis_edges:
        copy.wait_send()
    flip_one.wait_send()
    flip_two.wait_send()


def finish(
    cfg, small_ref, split_ref, one_ref,
    one_hbm, two_hbm, coef_one_hbm, coef_two_hbm,
    two_ref, cut_one_ref, cut_two_ref, store_sem,
):
    _, _, blocks, width, _, _, vecs, kept, _ = cfg
    span_one = kept + vecs
    span_two = span_one + vecs
    pieces = 8
    size = blocks // pieces * width
    stores = [pltpu.make_async_copy(one_ref, one_hbm.at[0], store_sem.at[0])]
    stores[-1].start()
    mixer = small_ref[pl.ds(2 * vecs, 2 * vecs), :].astype(BF16)[:, :2 * (span_two + vecs)]
    for piece in range(pieces):
        part = pl.ds(piece * size, size)
        out = dot(mixer, split_ref[:, part], NN)
        two_ref[:, part] = out[:vecs] + out[vecs:]
        stores.append(pltpu.make_async_copy(
            two_ref.at[:, part], two_hbm.at[0, :, part], store_sem.at[1 + piece]))
        stores[-1].start()
    cut_one_ref[...] = small_ref[pl.ds(0, vecs), :span_one + vecs]
    cut_two_ref[...] = small_ref[pl.ds(vecs, vecs), :span_two + vecs]
    stores.append(pltpu.make_async_copy(cut_one_ref, coef_one_hbm, store_sem.at[1 + pieces]))
    stores.append(pltpu.make_async_copy(cut_two_ref, coef_two_hbm, store_sem.at[2 + pieces]))
    for copy in stores[-2:]:
        copy.start()
    for copy in stores:
        copy.wait()


def per_device(
    vectors, basis, potential, hop_table, soc_table, nbr_block, nbr_type, nbr_count, flip_block
):
    blocks, slots = nbr_block.shape
    types, width, _ = hop_table.shape
    vecs, kept = vectors.shape[1], basis.shape[1]
    dom_total = lax.axis_size("dom")
    group_doms = 4 if dom_total % 4 == 0 else 1
    groups = dom_total // group_doms
    norm = float(2 * blocks * width * dom_total)
    cfg = (dom_total, group_doms, blocks, width, types, slots, vecs, kept, norm)
    count = blocks * width
    pair = 2 * vecs
    span_one, span_two = kept + vecs, kept + 2 * vecs
    kinds = (types + 1) * blocks
    vmem = pl.BlockSpec(memory_space=pltpu.VMEM)
    hbm = pl.BlockSpec(memory_space=pltpu.HBM)
    dma = pltpu.SemaphoreType.DMA
    shape = jax.ShapeDtypeStruct
    one, parts, small = pl.pallas_call(
        functools.partial(kernel, cfg),
        name="krylov",
        out_shape=(
            pltpu.VMEM((vecs, count), F32),
            pltpu.VMEM((2 * (span_two + vecs), count), BF16),
            pltpu.VMEM((4 * vecs, width), F32),
        ),
        in_specs=[hbm] * 9,
        out_specs=(vmem, vmem, vmem),
        scratch_shapes=[
            pltpu.VMEM((vecs, count), F32),
            pltpu.VMEM((kept, count), F32),
            pltpu.VMEM((1, count), F32),
            pltpu.VMEM((types * width, width), BF16),
            pltpu.VMEM(soc_table.shape, BF16),
            pltpu.VMEM((slots, blocks), I32),
            pltpu.VMEM((slots, blocks), I32),
            pltpu.VMEM((1, blocks), I32),
            pltpu.VMEM((1, blocks), I32),
            pltpu.VMEM((blocks * vecs, width), F32),
            pltpu.VMEM((2 * span_two, 2 * RANGE * width), BF16),
            pltpu.VMEM((2, vecs, blocks, width), BF16),
            pltpu.VMEM((2, vecs, blocks, width), BF16),
            pltpu.VMEM((2 * RANGE * vecs, width), F32),
            pltpu.VMEM((vecs, 2 * RANGE, width), BF16),
            pltpu.VMEM((vecs // 2, 2 * kinds, 2 * width), BF16),
            pltpu.VMEM((vecs // 2, 4 * RANGE * types, 2 * width), BF16),
            pltpu.VMEM((blocks, 2 * kinds), BF16),
            pltpu.VMEM((2 * RANGE, 4 * RANGE * types), BF16),
            pltpu.VMEM((vecs, width), F32),
            pltpu.VMEM((2, 2 * group_doms, vecs, width), F32),
            pltpu.VMEM((2, groups, vecs, width), F32),
            dma((9,)),
            dma((2,)), dma((2,)),
            dma((3, 2)), dma((3, 2)),
            dma((2, 2 * group_doms)), dma((2, 2 * group_doms)),
            dma((2, groups)), dma((2, groups)),
        ],
        compiler_params=pltpu.CompilerParams(
            collective_id=0, has_side_effects=True, vmem_limit_bytes=32 * 1024 * 1024),
    )(*[pltpu.with_memory_space_constraint(value, pltpu.HBM) for value in (
        vectors, basis, potential, hop_table.reshape(types * width, width), soc_table,
        nbr_block.T, nbr_type.T, nbr_count.reshape(1, blocks), flip_block.reshape(1, blocks))])
    one, two, coef_one, coef_two = pl.pallas_call(
        functools.partial(finish, cfg),
        name="finish",
        out_shape=(
            shape((1, vecs, count), F32),
            shape((1, vecs, count), F32),
            shape((vecs, span_one + vecs), F32),
            shape((vecs, span_two + vecs), F32),
        ),
        in_specs=[vmem, vmem, vmem],
        out_specs=(hbm,) * 4,
        scratch_shapes=[
            pltpu.VMEM((vecs, count), F32),
            pltpu.VMEM((vecs, span_one + vecs), F32),
            pltpu.VMEM((vecs, span_two + vecs), F32),
            dma((11,)),
        ],
        compiler_params=pltpu.CompilerParams(vmem_limit_bytes=16 * 1024 * 1024),
    )(small, parts, one)
    return one, two, coef_one.T, coef_two.T


def solution(mesh):
    return jax.shard_map(
        per_device,
        mesh=mesh,
        in_specs=(
            P("spin", None, "dom"),
            P("spin", None, "dom"),
            P("spin", "dom"),
            P(),
            P(),
            P("dom", None),
            P("dom", None),
            P("dom"),
            P("dom"),
        ),
        out_specs=(P("spin", None, "dom"), P("spin", None, "dom"), P(), P()),
        check_vma=False,
    )
```

```python
import functools
import jax
import jax.numpy as jnp
from jax import lax
from jax.experimental import pallas as pl
from jax.experimental.pallas import tpu as pltpu
from jax.sharding import PartitionSpec as P

RANGE = 8
STRIDE = 32
CHUNK = 16
MESH = pl.DeviceIdType.MESH
NT = (((1,), (1,)), ((), ()))
NN = (((1,), (0,)), ((), ()))
F32, BF16, I32 = jnp.float32, jnp.bfloat16, jnp.int32


def high_dot(left, right, dims):
    return lax.dot_general(
        left, right, dims, precision=lax.Precision.HIGHEST, preferred_element_type=F32
    )


def dot(left, right, dims):
    return lax.dot_general(left, right, dims, preferred_element_type=F32)


def split(value):
    low = value - value.astype(BF16).astype(F32)
    return jnp.concatenate([value, low], axis=0).astype(BF16)


def halves(value):
    high = value.astype(BF16)
    return high, (value - high.astype(F32)).astype(BF16)


def kernel(
    cfg,
    vec_hbm, basis_hbm, pot_hbm, hop_hbm, soc_hbm, nbr_hbm, type_hbm, count_hbm, flip_hbm,
    one_ref, split_ref, small_ref,
    vec_ref, basis_ref, pot_ref, hop_ref, soc_ref, nbr_ref, type_ref, count_ref, fliploc_ref,
    block_ref, edge_ref, major_ref, other_ref, near_ref, far_ref, prod_ref, edge_prod_ref,
    select_ref, edge_select_ref, fold_ref, weight_ref, stage_a_ref, stage_b_ref,
    all_one_ref, all_two_ref,
    load_sem, flip_send, flip_recv, edge_send, edge_recv, a_send, a_recv, b_send, b_recv,
    all_send, all_recv,
):
    dom_total, group_doms, blocks, width, types, slots, vecs, kept, norm, direct = cfg
    pair = 2 * vecs
    kept_groups = kept // vecs
    span_one = kept + vecs
    span_two = span_one + vecs
    rows_one = 2 * span_one
    rows_two = 2 * span_two
    kinds = types + 1
    devices = 2 * dom_total

    sources = [
        (vec_hbm.at[0], vec_ref), (nbr_hbm, nbr_ref), (type_hbm, type_ref),
        (count_hbm, count_ref), (flip_hbm, fliploc_ref), (basis_hbm.at[0], basis_ref),
        (hop_hbm, hop_ref), (soc_hbm, soc_ref), (pot_hbm, pot_ref)]
    loads = [
        pltpu.make_async_copy(src, dst, load_sem.at[n]) for n, (src, dst) in enumerate(sources)]
    for copy in loads:
        copy.start()
    groups = dom_total // group_doms
    group_size = 2 * group_doms
    dom, spin = lax.axis_index("dom"), lax.axis_index("spin")
    rank_a = (dom % group_doms) * 2 + spin
    rank_b = dom // group_doms
    dom_base = rank_b * group_doms
    left, right = (dom + dom_total - 1) % dom_total, (dom + 1) % dom_total

    def peer_a(shift):
        other = (rank_a + shift) % group_size
        return (dom_base + other // 2, other % 2)

    def peer_b(shift):
        return (((rank_b + shift) % groups) * group_doms + dom % group_doms, spin)

    far_first = sorted(range(dom_total), key=lambda shift: -min(shift, dom_total - shift))

    def everyone():
        for shift in far_first:
            ahead = dom + shift
            target = jnp.where(ahead >= dom_total, ahead - dom_total, ahead)
            if shift:
                yield (target, spin)
            yield (target, 1 - spin)

    barrier = pltpu.get_barrier_semaphore()
    if direct:
        greeted = list(everyone())
    else:
        greeted = [peer_a(shift) for shift in range(1, group_size)]
        greeted += [peer_b(shift) for shift in range(1, groups)]
        greeted += [(left, spin), (right, spin)]
    for target in greeted:
        pl.semaphore_signal(barrier, inc=1, device_id=target, device_id_type=MESH)

    lane = lax.broadcasted_iota(I32, (vecs, width), 1)
    row = lax.broadcasted_iota(I32, (vecs, width), 0)

    def cols(tile, size=1):
        return pl.ds(pl.multiple_of(tile * width, width), size * width)

    def flip_copy(app):
        return pltpu.make_async_remote_copy(
            src_ref=major_ref.at[app], dst_ref=other_ref.at[app],
            send_sem=flip_send.at[app], recv_sem=flip_recv.at[app],
            device_id=(dom, 1 - spin), device_id_type=MESH)

    def edge_copies(n, first, rows):
        part = pl.ds(first, rows)
        tail = pltpu.make_async_remote_copy(
            src_ref=split_ref.at[pl.ds(blocks - RANGE, RANGE), part],
            dst_ref=edge_ref.at[pl.ds(0, RANGE), part],
            send_sem=edge_send.at[n, 0], recv_sem=edge_recv.at[n, 0],
            device_id=(right, spin), device_id_type=MESH)
        head = pltpu.make_async_remote_copy(
            src_ref=split_ref.at[pl.ds(0, RANGE), part],
            dst_ref=edge_ref.at[pl.ds(RANGE, RANGE), part],
            send_sem=edge_send.at[n, 1], recv_sem=edge_recv.at[n, 1],
            device_id=(left, spin), device_id_type=MESH)
        return tail, head

    def to_major(value, scratch, base, store):
        for b, piece in enumerate(value):
            scratch[pl.ds(base + b * vecs, vecs), :] = piece
        for k in range(vecs):
            store(k, scratch[pl.ds(base + k, CHUNK, stride=vecs), :].astype(BF16))

    def tree(parts):
        while len(parts) > 1:
            parts = [sum(parts[p + 1:p + 2], parts[p]) for p in range(0, len(parts), 2)]
        return parts[0]

    def stage(n, ref, send, recv, rank, size, peer):
        def copy(shift, slot):
            return pltpu.make_async_remote_copy(
                src_ref=ref.at[n, rank], dst_ref=ref.at[n, slot],
                send_sem=send.at[n, shift], recv_sem=recv.at[n, slot],
                device_id=peer(shift), device_id_type=MESH)

        def begin(value):
            ref[n, rank] = value
            for shift in range(1, size):
                copy(shift, rank).start()

        def end():
            for shift in range(1, size):
                copy(shift, (rank + size - shift) % size).wait_recv()
            for shift in range(1, size):
                copy(shift, rank).wait_send()
            return tree([ref[n, slot] for slot in range(size)])
        return begin, end

    def staged(n):
        begin_a, end_a = stage(n, stage_a_ref, a_send, a_recv, rank_a, group_size, peer_a)
        begin_b, end_b = stage(n, stage_b_ref, b_send, b_recv, rank_b, groups, peer_b)
        return begin_a, lambda: begin_b(end_a()), end_b

    def share(n, ref, value, size, work):
        if not direct:
            begin, middle, end = staged(n)
            begin(value)
            done = work()
            middle()
            return end() * (1.0 / norm), done
        per = width // size
        rows = -(-vecs // per)
        out = value
        for q in range(1, per):
            moved = pltpu.roll(pltpu.roll(value, (-q * rows) % vecs, 0), q * size, 1)
            out = jnp.where((lane >= q * size) & (lane < (q + 1) * size), moved, out)
        me = dom * 2 + spin
        ref[me] = out[:rows]
        for target in everyone():
            pltpu.make_async_remote_copy(
                src_ref=ref.at[me], dst_ref=ref.at[me],
                send_sem=all_send.at[n], recv_sem=all_recv.at[n],
                device_id=target, device_id_type=MESH).start()
        done = work()
        others = ref.at[pl.ds(0, devices - 1)]
        whole = pltpu.make_async_remote_copy(
            src_ref=others, dst_ref=others, send_sem=all_send.at[n], recv_sem=all_recv.at[n],
            device_id=(dom, 1 - spin), device_id_type=MESH)
        whole.wait_recv()
        whole.wait_send()
        fold_ref[pl.ds(0, rows), :] = tree([ref[slot] for slot in range(devices)])
        total = fold_ref[...] * (1.0 / norm)
        out = jnp.where((lane < size) & (row < rows), total, 0.0)
        for q in range(1, per):
            moved = pltpu.roll(pltpu.roll(total, (q * rows) % vecs, 0), width - q * size, 1)
            out = jnp.where((lane < size) & (row >= q * rows) & (row < (q + 1) * rows), moved, out)
        return out, done

    def lanes(value, start, size):
        moved = value if start == 0 else pltpu.roll(value, width - start, 1)
        return jnp.where(lane < size, moved, 0.0)

    def tall(pieces):
        pad = width - vecs * len(pieces)
        return jnp.concatenate(list(pieces) + [jnp.zeros((pad, width), F32)], axis=0)

    def folded(value):
        wide = value.shape[1]
        fold_ref[:, pl.ds(0, wide)] = value[:vecs] + value[vecs:]
        both = fold_ref[...]
        both = both + pltpu.roll(both, width - vecs, 1)
        out = jnp.where(lane < vecs, both, 0.0)
        for g in range(1, wide // pair):
            inside = (lane >= vecs * g) & (lane < vecs * (g + 1))
            out = jnp.where(inside, pltpu.roll(both, width - vecs * g, 1), out)
        return out

    def wide_rows(ref, first, rows, tiles):
        return jnp.concatenate([ref[tile, pl.ds(first, rows), :] for tile in tiles], axis=1)

    def gram(first, rows, size, tiles):
        return dot(
            wide_rows(split_ref, first, rows, tiles), wide_rows(split_ref, 0, size, tiles), NT)

    def prepare(span_gram, count):
        eye = jnp.where(wide_row == wide_lane, 1.0, 0.0)
        once = 2.0 * eye - span_gram
        left_over = high_dot(eye - span_gram, eye - span_gram, NN)
        square = once + high_dot(left_over, once, NN)
        for n, table in enumerate([once, square, left_over][:count]):
            high, low = halves(table)
            weight_ref[n, :, pl.ds(0, width)] = high
            weight_ref[n, :, pl.ds(width, width)] = low

    def factor(first_t, image_gram, span_count, count):
        first = split(first_t)
        mixed = []
        for n in range(count):
            out = dot(first, weight_ref[n], NN)
            out = out[:vecs] + out[vecs:]
            mixed.append(out[:, :width] + out[:, width:])
        total_t = mixed[0]
        out = dot(split(mixed[1]), first, NT)
        fold_ref[:, pl.ds(0, pair)] = out[:vecs] + out[vecs:]
        both = fold_ref[...]
        square = image_gram - both - pltpu.roll(both, width - vecs, 1)
        table = jnp.where(lane < vecs, square, jnp.where(lane == row + vecs, 1.0, 0.0))
        table = table - pltpu.roll(total_t, pair, 1)
        if count > 2:
            table = table + pltpu.roll(mixed[2], pair + span_count, 1)
        lower = jnp.zeros((vecs, width), F32)
        for j in range(vecs):
            column = jnp.broadcast_to(table[:, j:j + 1], (vecs, width))
            pivot_row = jnp.broadcast_to(table[j:j + 1, :], (vecs, width))
            pivot = jnp.broadcast_to(column[j:j + 1, :], (vecs, width))
            scale = lax.rsqrt(pivot)
            column = column * scale
            lower = jnp.where((lane == j) & (row >= j), column, lower)
            pivot_row = pivot_row * scale
            table = jnp.where(
                row == j, pivot_row, jnp.where(row > j, table - column * pivot_row, table))
        mixer = jnp.zeros((vecs, width), F32)
        for g in range(span_count // vecs + 1):
            source = pair + vecs * g if g < span_count // vecs else vecs
            moved = pltpu.roll(table, (pair * g - source) % width, 1)
            mixer = jnp.where((lane >= pair * g) & (lane < pair * g + vecs), moved, mixer)
        mixer = mixer + pltpu.roll(mixer, vecs, 1)
        low = mixer - mixer.astype(BF16).astype(F32)
        return (
            total_t + pltpu.roll(lower, span_count, 1), jnp.concatenate([mixer, low], axis=0), table)

    def split_products(out, k, base, half_size, size, ref):
        high, low = halves(out)
        ref[k, pl.ds(base, size), :] = high
        ref[k, pl.ds(half_size + base, size), :] = low

    def products(app):
        def body(two, carry):
            weights = hop_ref[pl.ds(pl.multiple_of(two * 2 * width, 2 * width), 2 * width), :]
            for k in range(vecs):
                out = dot(major_ref[app, k], weights, NT)
                for half in range(2):
                    at = pl.multiple_of((two * 2 + half) * blocks, blocks)
                    split_products(
                        out[:, half * width:(half + 1) * width], k, at, kinds * blocks, blocks,
                        prod_ref)
            return carry
        lax.fori_loop(0, types // 2, body, 0)

    def flip_products(app):
        for k in range(vecs):
            out = dot(other_ref[app, k], soc_ref[spin], NT)
            split_products(out, k, types * blocks, kinds * blocks, blocks, prod_ref)

    def gather():
        def body(two, carry):
            chosen = jnp.concatenate([select_ref[n % kinds] for n in range(2 * kinds)], axis=1)
            held = jnp.concatenate([prod_ref[2 * two], prod_ref[2 * two + 1]], axis=1)
            out = dot(chosen, held, NN)
            for half in range(2):
                for i in range(blocks // vecs):
                    block_ref[pl.ds(i * vecs * vecs + 2 * two + half, vecs, stride=vecs), :] = (
                        out[i * vecs:(i + 1) * vecs, half * width:(half + 1) * width])
            return carry
        lax.fori_loop(0, vecs // 2, body, 0)

    def edge_gather():
        reach = 2 * RANGE
        source = far_ref[...].reshape(vecs * reach, width)

        for two in range(types // 2):
            out = dot(source, hop_ref[pl.ds(two * 2 * width, 2 * width), :], NT)
            for half in range(2):
                for k in range(vecs):
                    split_products(
                        out[k * reach:(k + 1) * reach, half * width:(half + 1) * width], k,
                        (two * 2 + half) * reach, types * reach, reach, edge_prod_ref)
        chosen = jnp.concatenate([edge_select_ref[...]] * 2, axis=1)
        for two in range(vecs // 2):
            held = jnp.concatenate([edge_prod_ref[2 * two], edge_prod_ref[2 * two + 1]], axis=1)
            out = dot(chosen, held, NN)
            for half in range(2):
                for end, base in enumerate((0, (blocks - RANGE) * vecs)):
                    at = pl.ds(base + 2 * two + half, RANGE, stride=vecs)
                    block_ref[at, :] = block_ref[at, :] + out[
                        end * RANGE:(end + 1) * RANGE, half * width:(half + 1) * width]

    def assemble(field_ref, first, low, high):
        def body(block, carry):
            image = pot_ref[pl.ds(0, 1), cols(block)] * field_ref[:, cols(block)]
            at = pl.multiple_of(block * vecs, vecs)
            image = image + block_ref[pl.ds(at, vecs), :]
            split_ref[block, pl.ds(first, pair), :] = split(image)
            return carry
        lax.fori_loop(low, high, body, 0, unroll=8)

    def chunk_pieces(value):
        return [value[:, b * width:(b + 1) * width] for b in range(CHUNK)]

    def store_major(app, chunk):
        def store(k, rounded):
            major_ref[app, k, pl.ds(pl.multiple_of(chunk * CHUNK, CHUNK), CHUNK), :] = rounded
        return store

    def round_body(chunk, carry):
        pieces = chunk_pieces(vec_ref[:, cols(chunk * CHUNK, CHUNK)])
        for b, piece in enumerate(pieces):
            split_ref[chunk * CHUNK + b, pl.ds(2 * kept, pair), :] = split(piece)
        to_major(pieces, block_ref, chunk * CHUNK * vecs, store_major(0, chunk))
        return carry

    def store_far(k, rounded):
        far_ref[k] = rounded

    wide_row = lax.broadcasted_iota(I32, (width, width), 0)
    wide_lane = lax.broadcasted_iota(I32, (width, width), 1)
    chunks = blocks // CHUNK
    loads[0].wait()
    round_body(0, 0)
    round_body(chunks - 1, 0)
    pl.semaphore_wait(barrier, len(greeted))
    vec_edges = edge_copies(0, 2 * kept, pair)
    for copy in vec_edges:
        copy.start()
    lax.fori_loop(1, chunks - 1, round_body, 0)
    flip_one = flip_copy(0)
    flip_one.start()
    for copy in loads[1:5]:
        copy.wait()

    local = lax.broadcasted_iota(I32, (slots, blocks), 1)
    slot_at = lax.broadcasted_iota(I32, (slots, blocks), 0)
    shift = nbr_ref[...] - (dom * blocks + local) + RANGE
    total = dom_total * blocks
    shift = jnp.where(shift < 0, shift + total, shift)
    shift = jnp.where(shift >= total, shift - total, shift)
    place = local + shift - RANGE
    live = slot_at < count_ref[...]
    inside = (place >= 0) & (place < blocks)
    code = jnp.where(live & inside, type_ref[...] * STRIDE + shift, -1)
    edge_code = jnp.where(place < 0, place + RANGE, place - blocks + RANGE)
    edge_code = jnp.where(live & ~inside, type_ref[...] * (2 * RANGE) + edge_code, -1)

    def counts(codes, base):
        wanted = row + base
        return tree([jnp.where(codes[s:s + 1, :] == wanted, 1.0, 0.0) for s in range(slots)])

    band = (wide_lane - wide_row <= RANGE) & (wide_row - wide_lane <= RANGE)
    per_tile = width // STRIDE
    blank = jnp.zeros((vecs, width), F32)
    for tile in range(types // per_tile):
        pieces = []
        for r in range(width // vecs):
            live_rows = (r * vecs) % STRIDE <= 2 * RANGE
            pieces.append(counts(code, tile * width + r * vecs) if live_rows else blank)
        table = jnp.concatenate(pieces, axis=0).T
        for t in range(per_tile):
            moved = pltpu.roll(
                table, (-RANGE - STRIDE * t) % width, 1, stride=1, stride_axis=0)
            select_ref[tile * per_tile + t] = jnp.where(band, moved, 0.0).astype(BF16)
    flip_local = fliploc_ref[...] - dom * blocks
    select_ref[types] = jnp.where(flip_local == wide_row, 1.0, 0.0).T.astype(BF16)
    table = jnp.concatenate(
        [counts(edge_code, r * vecs) for r in range(width // vecs)], axis=0).T
    edge_select_ref[...] = jnp.concatenate(
        [table[:RANGE], table[blocks - RANGE:]], axis=0).astype(BF16)
    fold_ref[...] = jnp.zeros((vecs, width), F32)

    loads[5].wait()

    def split_basis(chunk, carry):
        for b in range(4):
            block = chunk * 4 + b
            for g in range(kept_groups):
                split_ref[block, pl.ds(g * pair, pair), :] = split(
                    basis_ref[pl.ds(g * vecs, vecs), cols(block)])
        return carry
    lax.fori_loop(0, blocks // 4, split_basis, 0, unroll=2)
    basis_edges = edge_copies(1, 0, 2 * kept)
    for copy in basis_edges:
        copy.start()
    low_gram = gram(0, rows_one, rows_one, range(blocks))
    packed_low = jnp.zeros((vecs, width), F32)
    for g in range(span_one // vecs):
        piece = folded(low_gram[g * pair:(g + 1) * pair])
        packed_low = packed_low + (pltpu.roll(piece, g * span_one, 1) if g else piece)
    low_begin, low_middle, low_end = staged(0)
    low_begin(packed_low)
    for copy in loads[6:]:
        copy.wait()

    products(0)
    low_middle()
    flip_one.wait_recv()
    flip_products(0)
    gather()
    assemble(vec_ref, rows_one, RANGE, blocks - RANGE)
    result = gram(rows_one, pair, rows_two, range(RANGE, blocks - RANGE))
    for copy in vec_edges:
        copy.wait_recv()
    to_major(
        [edge_ref[b, pl.ds(2 * kept, pair), :].astype(F32)[:vecs] for b in range(2 * RANGE)],
        near_ref, 0, store_far)
    edge_gather()
    assemble(vec_ref, rows_one, 0, RANGE)
    assemble(vec_ref, rows_one, blocks - RANGE, blocks)
    image_edges = edge_copies(2, rows_one, pair)
    ends = list(range(RANGE)) + list(range(blocks - RANGE, blocks))
    result = folded(result + gram(rows_one, pair, rows_two, ends))

    def while_sharing():
        for copy in image_edges:
            copy.start()
        packed = low_end() * (1.0 / norm)
        span_gram = tall(
            [lanes(packed, g * span_one, span_one) for g in range(span_one // vecs)])
        prepare(span_gram, 3)
        return span_gram
    packed, span_gram = share(1, all_one_ref, result, span_one + vecs, while_sharing)
    coefs, mixer, table = factor(
        lanes(packed, 0, span_one), lanes(packed, span_one, vecs), span_one, 3)
    small_ref[pl.ds(0, vecs), :] = coefs
    mixer = mixer.astype(BF16)[:, :rows_two]
    for copy in image_edges:
        copy.wait_send()

    def mix_body(chunk, carry):
        out = dot(
            mixer, wide_rows(split_ref, 0, rows_two, [chunk * CHUNK + b for b in range(CHUNK)]), NN)
        value = out[:vecs] + out[vecs:]
        one_ref[:, cols(chunk * CHUNK, CHUNK)] = value
        pieces = chunk_pieces(value)
        for b, piece in enumerate(pieces):
            split_ref[chunk * CHUNK + b, pl.ds(rows_one, pair), :] = split(piece)
        to_major(pieces, block_ref, chunk * CHUNK * vecs, store_major(1, chunk))
        return carry
    lax.fori_loop(0, chunks, mix_body, 0)
    flip_two = flip_copy(1)
    flip_two.start()
    products(1)
    for copy in image_edges + basis_edges:
        copy.wait_recv()
    out = dot(mixer, wide_rows(edge_ref, 0, rows_two, range(2 * RANGE)), NN)
    to_major(chunk_pieces(out[:vecs] + out[vecs:]), near_ref, 0, store_far)
    flip_two.wait_recv()
    flip_products(1)
    gather()
    edge_gather()
    assemble(one_ref, rows_two, 0, blocks)
    result = folded(gram(rows_two, pair, rows_two + pair, range(blocks)))

    def while_sharing_two():
        cross = lanes(table, pair + span_one, span_one)
        cross = cross + jnp.where(lane == row + span_one, 1.0, 0.0)
        low = jnp.concatenate(
            [jnp.zeros((span_one, width), F32), cross,
             jnp.zeros((width - span_two, width), F32)], axis=0)
        prepare(span_gram + low + jnp.where(
            (wide_row < span_one) & (wide_lane >= span_one), low.T, 0.0), 2)
        for copy in vec_edges + basis_edges:
            copy.wait_send()
        flip_one.wait_send()
        flip_two.wait_send()
    packed, _ = share(2, all_two_ref, result, span_two + vecs, while_sharing_two)
    coefs, mixer, _ = factor(
        lanes(packed, 0, span_two), lanes(packed, span_two, vecs), span_two, 2)
    small_ref[pl.ds(vecs, vecs), :] = coefs
    small_ref[pl.ds(pair, pair), :] = mixer


def finish(
    cfg, small_ref, split_ref, one_ref,
    one_hbm, two_hbm, coef_one_hbm, coef_two_hbm,
    two_ref, cut_one_ref, cut_two_ref, store_sem,
):
    _, _, blocks, width, _, _, vecs, kept, _, _ = cfg
    span_one = kept + vecs
    span_two = span_one + vecs
    pieces = 8
    size = blocks // pieces * width
    stores = [pltpu.make_async_copy(one_ref, one_hbm.at[0], store_sem.at[0])]
    stores[-1].start()
    mixer = small_ref[pl.ds(2 * vecs, 2 * vecs), :].astype(BF16)[:, :2 * (span_two + vecs)]
    for piece in range(pieces):
        part = pl.ds(piece * size, size)
        tiles = range(piece * (blocks // pieces), (piece + 1) * (blocks // pieces))
        out = dot(mixer, jnp.concatenate([split_ref[tile] for tile in tiles], axis=1), NN)
        two_ref[:, part] = out[:vecs] + out[vecs:]
        stores.append(pltpu.make_async_copy(
            two_ref.at[:, part], two_hbm.at[0, :, part], store_sem.at[1 + piece]))
        stores[-1].start()
    cut_one_ref[...] = small_ref[pl.ds(0, vecs), :span_one + vecs]
    cut_two_ref[...] = small_ref[pl.ds(vecs, vecs), :span_two + vecs]
    stores.append(pltpu.make_async_copy(cut_one_ref, coef_one_hbm, store_sem.at[1 + pieces]))
    stores.append(pltpu.make_async_copy(cut_two_ref, coef_two_hbm, store_sem.at[2 + pieces]))
    for copy in stores[-2:]:
        copy.start()
    for copy in stores:
        copy.wait()


def per_device(
    vectors, basis, potential, hop_table, soc_table, nbr_block, nbr_type, nbr_count, flip_block
):
    blocks, slots = nbr_block.shape
    types, width, _ = hop_table.shape
    vecs, kept = vectors.shape[1], basis.shape[1]
    dom_total = lax.axis_size("dom")
    group_doms = 4 if dom_total % 4 == 0 else 1
    groups = dom_total // group_doms
    norm = float(2 * blocks * width * dom_total)
    direct = dom_total <= 32
    cfg = (dom_total, group_doms, blocks, width, types, slots, vecs, kept, norm, direct)
    count = blocks * width
    pair = 2 * vecs
    span_one, span_two = kept + vecs, kept + 2 * vecs
    kinds = types + 1
    seats = 2 * dom_total if direct else 1
    row_count = lambda size: -(-vecs // (width // size))
    vmem = pl.BlockSpec(memory_space=pltpu.VMEM)
    hbm = pl.BlockSpec(memory_space=pltpu.HBM)
    dma = pltpu.SemaphoreType.DMA
    shape = jax.ShapeDtypeStruct
    one, parts, small = pl.pallas_call(
        functools.partial(kernel, cfg),
        name="krylov",
        out_shape=(
            pltpu.VMEM((vecs, count), F32),
            pltpu.VMEM((blocks, 2 * (span_two + vecs), width), BF16),
            pltpu.VMEM((4 * vecs, width), F32),
        ),
        in_specs=[hbm] * 9,
        out_specs=(vmem, vmem, vmem),
        scratch_shapes=[
            pltpu.VMEM((vecs, count), F32),
            pltpu.VMEM((kept, count), F32),
            pltpu.VMEM((1, count), F32),
            pltpu.VMEM((types * width, width), BF16),
            pltpu.VMEM(soc_table.shape, BF16),
            pltpu.VMEM((slots, blocks), I32),
            pltpu.VMEM((slots, blocks), I32),
            pltpu.VMEM((1, blocks), I32),
            pltpu.VMEM((1, blocks), I32),
            pltpu.VMEM((blocks * vecs, width), F32),
            pltpu.VMEM((2 * RANGE, 2 * span_two, width), BF16),
            pltpu.VMEM((2, vecs, blocks, width), BF16),
            pltpu.VMEM((2, vecs, blocks, width), BF16),
            pltpu.VMEM((2 * RANGE * vecs, width), F32),
            pltpu.VMEM((vecs, 2 * RANGE, width), BF16),
            pltpu.VMEM((vecs, 2 * kinds * blocks, width), BF16),
            pltpu.VMEM((vecs, 4 * RANGE * types, width), BF16),
            pltpu.VMEM((kinds, blocks, width), BF16),
            pltpu.VMEM((2 * RANGE, 2 * RANGE * types), BF16),
            pltpu.VMEM((vecs, width), F32),
            pltpu.VMEM((3, width, 2 * width), BF16),
            pltpu.VMEM((3, 2 * group_doms, vecs, width), F32),
            pltpu.VMEM((3, groups, vecs, width), F32),
            pltpu.VMEM((seats, row_count(span_one + vecs), width), F32),
            pltpu.VMEM((seats, row_count(span_two + vecs), width), F32),
            dma((9,)),
            dma((2,)), dma((2,)),
            dma((3, 2)), dma((3, 2)),
            dma((3, 2 * group_doms)), dma((3, 2 * group_doms)),
            dma((3, groups)), dma((3, groups)),
            dma((3,)), dma((3,)),
        ],
        compiler_params=pltpu.CompilerParams(
            collective_id=0, has_side_effects=True, vmem_limit_bytes=32 * 1024 * 1024),
    )(*[pltpu.with_memory_space_constraint(value, pltpu.HBM) for value in (
        vectors, basis, potential, hop_table.reshape(types * width, width), soc_table,
        nbr_block.T, nbr_type.T, nbr_count.reshape(1, blocks), flip_block.reshape(1, blocks))])
    one, two, coef_one, coef_two = pl.pallas_call(
        functools.partial(finish, cfg),
        name="finish",
        out_shape=(
            shape((1, vecs, count), F32),
            shape((1, vecs, count), F32),
            shape((vecs, span_one + vecs), F32),
            shape((vecs, span_two + vecs), F32),
        ),
        in_specs=[vmem, vmem, vmem],
        out_specs=(hbm,) * 4,
        scratch_shapes=[
            pltpu.VMEM((vecs, count), F32),
            pltpu.VMEM((vecs, span_one + vecs), F32),
            pltpu.VMEM((vecs, span_two + vecs), F32),
            dma((11,)),
        ],
        compiler_params=pltpu.CompilerParams(vmem_limit_bytes=16 * 1024 * 1024),
    )(small, parts, one)
    return one, two, coef_one.T, coef_two.T


def solution(mesh):
    return jax.shard_map(
        per_device,
        mesh=mesh,
        in_specs=(
            P("spin", None, "dom"),
            P("spin", None, "dom"),
            P("spin", "dom"),
            P(),
            P(),
            P("dom", None),
            P("dom", None),
            P("dom"),
            P("dom"),
        ),
        out_specs=(P("spin", None, "dom"), P("spin", None, "dom"), P(), P()),
        check_vma=False,
    )
```

```python
import functools
import jax
import jax.numpy as jnp
from jax import lax
from jax.experimental import pallas as pl
from jax.experimental.pallas import tpu as pltpu
from jax.sharding import PartitionSpec as P

RANGE = 8
STRIDE = 32
CHUNK = 16
MESH = pl.DeviceIdType.MESH
NT = (((1,), (1,)), ((), ()))
NN = (((1,), (0,)), ((), ()))
F32, BF16, I32 = jnp.float32, jnp.bfloat16, jnp.int32


def high_dot(left, right, dims):
    return lax.dot_general(
        left, right, dims, precision=lax.Precision.HIGHEST, preferred_element_type=F32
    )


def dot(left, right, dims):
    return lax.dot_general(left, right, dims, preferred_element_type=F32)


def split(value):
    low = value - value.astype(BF16).astype(F32)
    return jnp.concatenate([value, low], axis=0).astype(BF16)


def halves(value):
    high = value.astype(BF16)
    return high, (value - high.astype(F32)).astype(BF16)


def kernel(
    cfg,
    vec_hbm, basis_hbm, pot_hbm, hop_hbm, soc_hbm, nbr_hbm, type_hbm, count_hbm, flip_hbm,
    one_ref, split_ref, small_ref,
    vec_ref, basis_ref, pot_ref, hop_ref, soc_ref, nbr_ref, type_ref, count_ref, fliploc_ref,
    block_ref, edge_ref, major_ref, other_ref, near_ref, far_ref, prod_ref, edge_prod_ref,
    select_ref, edge_select_ref, fold_ref, weight_ref, stage_a_ref, stage_b_ref,
    all_low_ref, all_one_ref, all_two_ref,
    load_sem, flip_send, flip_recv, edge_send, edge_recv, a_send, a_recv, b_send, b_recv,
    all_send, all_recv,
):
    dom_total, group_doms, blocks, width, types, slots, vecs, kept, norm, direct = cfg
    pair = 2 * vecs
    kept_groups = kept // vecs
    span_one = kept + vecs
    span_two = span_one + vecs
    rows_one = 2 * span_one
    rows_two = 2 * span_two
    kinds = types + 1
    devices = 2 * dom_total

    sources = [
        (vec_hbm.at[0], vec_ref), (nbr_hbm, nbr_ref), (type_hbm, type_ref),
        (count_hbm, count_ref), (flip_hbm, fliploc_ref), (basis_hbm.at[0], basis_ref),
        (hop_hbm, hop_ref), (soc_hbm, soc_ref), (pot_hbm, pot_ref)]
    loads = [
        pltpu.make_async_copy(src, dst, load_sem.at[n]) for n, (src, dst) in enumerate(sources)]
    for copy in loads:
        copy.start()
    groups = dom_total // group_doms
    group_size = 2 * group_doms
    dom, spin = lax.axis_index("dom"), lax.axis_index("spin")
    rank_a = (dom % group_doms) * 2 + spin
    rank_b = dom // group_doms
    dom_base = rank_b * group_doms
    left, right = (dom + dom_total - 1) % dom_total, (dom + 1) % dom_total

    def peer_a(shift):
        other = (rank_a + shift) % group_size
        return (dom_base + other // 2, other % 2)

    def peer_b(shift):
        return (((rank_b + shift) % groups) * group_doms + dom % group_doms, spin)

    far_first = sorted(range(dom_total), key=lambda shift: -min(shift, dom_total - shift))

    def everyone():
        for shift in far_first:
            ahead = dom + shift
            target = jnp.where(ahead >= dom_total, ahead - dom_total, ahead)
            if shift:
                yield (target, spin)
            yield (target, 1 - spin)

    barrier = pltpu.get_barrier_semaphore()
    if direct:
        greeted = list(everyone())
    else:
        greeted = [peer_a(shift) for shift in range(1, group_size)]
        greeted += [peer_b(shift) for shift in range(1, groups)]
        greeted += [(left, spin), (right, spin)]
    for target in greeted:
        pl.semaphore_signal(barrier, inc=1, device_id=target, device_id_type=MESH)

    lane = lax.broadcasted_iota(I32, (vecs, width), 1)
    row = lax.broadcasted_iota(I32, (vecs, width), 0)

    def cols(tile, size=1):
        return pl.ds(pl.multiple_of(tile * width, width), size * width)

    def flip_copy(app):
        return pltpu.make_async_remote_copy(
            src_ref=major_ref.at[app], dst_ref=other_ref.at[app],
            send_sem=flip_send.at[app], recv_sem=flip_recv.at[app],
            device_id=(dom, 1 - spin), device_id_type=MESH)

    def edge_copies(n, first, rows):
        part = pl.ds(first, rows)
        tail = pltpu.make_async_remote_copy(
            src_ref=split_ref.at[pl.ds(blocks - RANGE, RANGE), part],
            dst_ref=edge_ref.at[pl.ds(0, RANGE), part],
            send_sem=edge_send.at[n, 0], recv_sem=edge_recv.at[n, 0],
            device_id=(right, spin), device_id_type=MESH)
        head = pltpu.make_async_remote_copy(
            src_ref=split_ref.at[pl.ds(0, RANGE), part],
            dst_ref=edge_ref.at[pl.ds(RANGE, RANGE), part],
            send_sem=edge_send.at[n, 1], recv_sem=edge_recv.at[n, 1],
            device_id=(left, spin), device_id_type=MESH)
        return tail, head

    def to_major(value, scratch, base, store):
        for b, piece in enumerate(value):
            scratch[pl.ds(base + b * vecs, vecs), :] = piece
        for k in range(vecs):
            store(k, scratch[pl.ds(base + k, CHUNK, stride=vecs), :].astype(BF16))

    def tree(parts):
        while len(parts) > 1:
            parts = [sum(parts[p + 1:p + 2], parts[p]) for p in range(0, len(parts), 2)]
        return parts[0]

    def stage(n, ref, send, recv, rank, size, peer):
        def copy(shift, slot):
            return pltpu.make_async_remote_copy(
                src_ref=ref.at[n, rank], dst_ref=ref.at[n, slot],
                send_sem=send.at[n, shift], recv_sem=recv.at[n, slot],
                device_id=peer(shift), device_id_type=MESH)

        def begin(value):
            ref[n, rank] = value
            for shift in range(1, size):
                copy(shift, rank).start()

        def end():
            for shift in range(1, size):
                copy(shift, (rank + size - shift) % size).wait_recv()
            for shift in range(1, size):
                copy(shift, rank).wait_send()
            return tree([ref[n, slot] for slot in range(size)])
        return begin, end

    def staged(n):
        begin_a, end_a = stage(n, stage_a_ref, a_send, a_recv, rank_a, group_size, peer_a)
        begin_b, end_b = stage(n, stage_b_ref, b_send, b_recv, rank_b, groups, peer_b)
        return begin_a, lambda: begin_b(end_a()), end_b

    def exchange(n, ref):
        if not direct:
            return staged(n)
        me = dom * 2 + spin

        def begin(value):
            ref[me] = value
            for target in everyone():
                pltpu.make_async_remote_copy(
                    src_ref=ref.at[me], dst_ref=ref.at[me],
                    send_sem=all_send.at[n], recv_sem=all_recv.at[n],
                    device_id=target, device_id_type=MESH).start()

        def end():
            others = ref.at[pl.ds(0, devices - 1)]
            whole = pltpu.make_async_remote_copy(
                src_ref=others, dst_ref=others, send_sem=all_send.at[n], recv_sem=all_recv.at[n],
                device_id=(dom, 1 - spin), device_id_type=MESH)
            whole.wait_recv()
            whole.wait_send()
            return tree([ref[slot] for slot in range(devices)])
        return begin, lambda: None, end

    def share(n, ref, value, size, work):
        begin, middle, end = exchange(n, ref)
        if not direct:
            begin(value)
            done = work()
            middle()
            return end() * (1.0 / norm), done
        per = width // size
        rows = -(-vecs // per)
        out = value
        for q in range(1, per):
            moved = pltpu.roll(pltpu.roll(value, (-q * rows) % vecs, 0), q * size, 1)
            out = jnp.where((lane >= q * size) & (lane < (q + 1) * size), moved, out)
        begin(out[:rows])
        done = work()
        fold_ref[pl.ds(0, rows), :] = end()
        total = fold_ref[...] * (1.0 / norm)
        out = jnp.where((lane < size) & (row < rows), total, 0.0)
        for q in range(1, per):
            moved = pltpu.roll(pltpu.roll(total, (q * rows) % vecs, 0), width - q * size, 1)
            out = jnp.where((lane < size) & (row >= q * rows) & (row < (q + 1) * rows), moved, out)
        return out, done

    def lanes(value, start, size):
        moved = value if start == 0 else pltpu.roll(value, width - start, 1)
        return jnp.where(lane < size, moved, 0.0)

    def tall(pieces):
        pad = width - vecs * len(pieces)
        return jnp.concatenate(list(pieces) + [jnp.zeros((pad, width), F32)], axis=0)

    def folded(value):
        wide = value.shape[1]
        fold_ref[:, pl.ds(0, wide)] = value[:vecs] + value[vecs:]
        both = fold_ref[...]
        both = both + pltpu.roll(both, width - vecs, 1)
        out = jnp.where(lane < vecs, both, 0.0)
        for g in range(1, wide // pair):
            inside = (lane >= vecs * g) & (lane < vecs * (g + 1))
            out = jnp.where(inside, pltpu.roll(both, width - vecs * g, 1), out)
        return out

    def wide_rows(ref, first, rows, tiles):
        return jnp.concatenate([ref[tile, pl.ds(first, rows), :] for tile in tiles], axis=1)

    def gram(first, rows, size, tiles):
        return dot(
            wide_rows(split_ref, first, rows, tiles), wide_rows(split_ref, 0, size, tiles), NT)

    def prepare(span_gram, count):
        eye = jnp.where(wide_row == wide_lane, 1.0, 0.0)
        once = 2.0 * eye - span_gram
        left_over = high_dot(eye - span_gram, eye - span_gram, NN)
        square = once + high_dot(left_over, once, NN)
        for n, table in enumerate([once, square, left_over][:count]):
            high, low = halves(table)
            weight_ref[n, :, pl.ds(0, width)] = high
            weight_ref[n, :, pl.ds(width, width)] = low

    def factor(first_t, image_gram, span_count, count):
        first = split(first_t)
        mixed = []
        for n in range(count):
            out = dot(first, weight_ref[n], NN)
            out = out[:vecs] + out[vecs:]
            mixed.append(out[:, :width] + out[:, width:])
        total_t = mixed[0]
        out = dot(split(mixed[1]), first, NT)
        fold_ref[:, pl.ds(0, pair)] = out[:vecs] + out[vecs:]
        both = fold_ref[...]
        square = image_gram - both - pltpu.roll(both, width - vecs, 1)
        table = jnp.where(lane < vecs, square, jnp.where(lane == row + vecs, 1.0, 0.0))
        table = table - pltpu.roll(total_t, pair, 1)
        if count > 2:
            table = table + pltpu.roll(mixed[2], pair + span_count, 1)
        lower = jnp.zeros((vecs, width), F32)
        for j in range(vecs):
            column = jnp.broadcast_to(table[:, j:j + 1], (vecs, width))
            pivot_row = jnp.broadcast_to(table[j:j + 1, :], (vecs, width))
            pivot = jnp.broadcast_to(column[j:j + 1, :], (vecs, width))
            scale = lax.rsqrt(pivot)
            column = column * scale
            lower = jnp.where((lane == j) & (row >= j), column, lower)
            pivot_row = pivot_row * scale
            table = jnp.where(
                row == j, pivot_row, jnp.where(row > j, table - column * pivot_row, table))
        mixer = jnp.zeros((vecs, width), F32)
        for g in range(span_count // vecs + 1):
            source = pair + vecs * g if g < span_count // vecs else vecs
            moved = pltpu.roll(table, (pair * g - source) % width, 1)
            mixer = jnp.where((lane >= pair * g) & (lane < pair * g + vecs), moved, mixer)
        mixer = mixer + pltpu.roll(mixer, vecs, 1)
        low = mixer - mixer.astype(BF16).astype(F32)
        return (
            total_t + pltpu.roll(lower, span_count, 1), jnp.concatenate([mixer, low], axis=0), table)

    def split_products(out, k, base, half_size, size, ref):
        high, low = halves(out)
        ref[k, pl.ds(base, size), :] = high
        ref[k, pl.ds(half_size + base, size), :] = low

    def products(app):
        def body(two, carry):
            weights = hop_ref[pl.ds(pl.multiple_of(two * 2 * width, 2 * width), 2 * width), :]
            for k in range(vecs):
                out = dot(major_ref[app, k], weights, NT)
                for half in range(2):
                    at = pl.multiple_of((two * 2 + half) * blocks, blocks)
                    split_products(
                        out[:, half * width:(half + 1) * width], k, at, kinds * blocks, blocks,
                        prod_ref)
            return carry
        lax.fori_loop(0, types // 2, body, 0, unroll=2)

    def flip_products(app):
        for k in range(vecs):
            out = dot(other_ref[app, k], soc_ref[spin], NT)
            split_products(out, k, types * blocks, kinds * blocks, blocks, prod_ref)

    def gather():
        def body(two, carry):
            chosen = jnp.concatenate([select_ref[n % kinds] for n in range(2 * kinds)], axis=1)
            held = jnp.concatenate([prod_ref[2 * two], prod_ref[2 * two + 1]], axis=1)
            out = dot(chosen, held, NN)
            for half in range(2):
                for i in range(blocks // vecs):
                    block_ref[pl.ds(i * vecs * vecs + 2 * two + half, vecs, stride=vecs), :] = (
                        out[i * vecs:(i + 1) * vecs, half * width:(half + 1) * width])
            return carry
        lax.fori_loop(0, vecs // 2, body, 0, unroll=2)

    def edge_gather():
        reach = 2 * RANGE
        source = far_ref[...].reshape(vecs * reach, width)

        for two in range(types // 2):
            out = dot(source, hop_ref[pl.ds(two * 2 * width, 2 * width), :], NT)
            for half in range(2):
                for k in range(vecs):
                    split_products(
                        out[k * reach:(k + 1) * reach, half * width:(half + 1) * width], k,
                        (two * 2 + half) * reach, types * reach, reach, edge_prod_ref)
        chosen = jnp.concatenate([edge_select_ref[...]] * 2, axis=1)
        for two in range(vecs // 2):
            held = jnp.concatenate([edge_prod_ref[2 * two], edge_prod_ref[2 * two + 1]], axis=1)
            out = dot(chosen, held, NN)
            for half in range(2):
                for end, base in enumerate((0, (blocks - RANGE) * vecs)):
                    at = pl.ds(base + 2 * two + half, RANGE, stride=vecs)
                    block_ref[at, :] = block_ref[at, :] + out[
                        end * RANGE:(end + 1) * RANGE, half * width:(half + 1) * width]

    def assemble(field_ref, first, low, high):
        def body(block, carry):
            image = pot_ref[pl.ds(0, 1), cols(block)] * field_ref[:, cols(block)]
            at = pl.multiple_of(block * vecs, vecs)
            image = image + block_ref[pl.ds(at, vecs), :]
            split_ref[block, pl.ds(first, pair), :] = split(image)
            return carry
        lax.fori_loop(low, high, body, 0, unroll=8)

    def chunk_pieces(value):
        return [value[:, b * width:(b + 1) * width] for b in range(CHUNK)]

    def store_major(app, chunk):
        def store(k, rounded):
            major_ref[app, k, pl.ds(pl.multiple_of(chunk * CHUNK, CHUNK), CHUNK), :] = rounded
        return store

    def round_body(chunk, carry):
        pieces = chunk_pieces(vec_ref[:, cols(chunk * CHUNK, CHUNK)])
        for b, piece in enumerate(pieces):
            split_ref[chunk * CHUNK + b, pl.ds(2 * kept, pair), :] = split(piece)
        to_major(pieces, block_ref, chunk * CHUNK * vecs, store_major(0, chunk))
        return carry

    def store_far(k, rounded):
        far_ref[k] = rounded

    wide_row = lax.broadcasted_iota(I32, (width, width), 0)
    wide_lane = lax.broadcasted_iota(I32, (width, width), 1)
    chunks = blocks // CHUNK
    loads[0].wait()
    round_body(0, 0)
    round_body(chunks - 1, 0)
    pl.semaphore_wait(barrier, len(greeted))
    vec_edges = edge_copies(0, 2 * kept, pair)
    for copy in vec_edges:
        copy.start()
    lax.fori_loop(1, chunks - 1, round_body, 0)
    flip_one = flip_copy(0)
    flip_one.start()
    for copy in loads[1:5]:
        copy.wait()

    local = lax.broadcasted_iota(I32, (slots, blocks), 1)
    slot_at = lax.broadcasted_iota(I32, (slots, blocks), 0)
    shift = nbr_ref[...] - (dom * blocks + local) + RANGE
    total = dom_total * blocks
    shift = jnp.where(shift < 0, shift + total, shift)
    shift = jnp.where(shift >= total, shift - total, shift)
    place = local + shift - RANGE
    live = slot_at < count_ref[...]
    inside = (place >= 0) & (place < blocks)
    code = jnp.where(live & inside, type_ref[...] * STRIDE + shift, -1)
    edge_code = jnp.where(place < 0, place + RANGE, place - blocks + RANGE)
    edge_code = jnp.where(live & ~inside, type_ref[...] * (2 * RANGE) + edge_code, -1)

    def counts(codes, base):
        wanted = row + base
        return tree([jnp.where(codes[s:s + 1, :] == wanted, 1.0, 0.0) for s in range(slots)])

    band = (wide_lane - wide_row <= RANGE) & (wide_row - wide_lane <= RANGE)
    per_tile = width // STRIDE
    blank = jnp.zeros((vecs, width), F32)
    for tile in range(types // per_tile):
        pieces = []
        for r in range(width // vecs):
            live_rows = (r * vecs) % STRIDE <= 2 * RANGE
            pieces.append(counts(code, tile * width + r * vecs) if live_rows else blank)
        table = jnp.concatenate(pieces, axis=0).T
        for t in range(per_tile):
            moved = pltpu.roll(
                table, (-RANGE - STRIDE * t) % width, 1, stride=1, stride_axis=0)
            select_ref[tile * per_tile + t] = jnp.where(band, moved, 0.0).astype(BF16)
    flip_local = fliploc_ref[...] - dom * blocks
    select_ref[types] = jnp.where(flip_local == wide_row, 1.0, 0.0).T.astype(BF16)
    table = jnp.concatenate(
        [counts(edge_code, r * vecs) for r in range(width // vecs)], axis=0).T
    edge_select_ref[...] = jnp.concatenate(
        [table[:RANGE], table[blocks - RANGE:]], axis=0).astype(BF16)
    fold_ref[...] = jnp.zeros((vecs, width), F32)

    loads[5].wait()

    def split_basis(chunk, carry):
        for b in range(4):
            block = chunk * 4 + b
            for g in range(kept_groups):
                split_ref[block, pl.ds(g * pair, pair), :] = split(
                    basis_ref[pl.ds(g * vecs, vecs), cols(block)])
        return carry
    lax.fori_loop(0, blocks // 4, split_basis, 0, unroll=2)
    basis_edges = edge_copies(1, 0, 2 * kept)
    for copy in basis_edges:
        copy.start()
    low_gram = gram(0, rows_one, rows_one, range(blocks))
    packed_low = jnp.zeros((vecs, width), F32)
    for g in range(span_one // vecs):
        piece = folded(low_gram[g * pair:(g + 1) * pair])
        packed_low = packed_low + (pltpu.roll(piece, g * span_one, 1) if g else piece)
    low_begin, low_middle, low_end = exchange(0, all_low_ref)
    low_begin(packed_low)
    for copy in loads[6:]:
        copy.wait()

    products(0)
    low_middle()
    flip_one.wait_recv()
    flip_products(0)
    gather()
    assemble(vec_ref, rows_one, RANGE, blocks - RANGE)
    result = gram(rows_one, pair, rows_two, range(RANGE, blocks - RANGE))
    for copy in vec_edges:
        copy.wait_recv()
    to_major(
        [edge_ref[b, pl.ds(2 * kept, pair), :].astype(F32)[:vecs] for b in range(2 * RANGE)],
        near_ref, 0, store_far)
    edge_gather()
    assemble(vec_ref, rows_one, 0, RANGE)
    assemble(vec_ref, rows_one, blocks - RANGE, blocks)
    image_edges = edge_copies(2, rows_one, pair)
    ends = list(range(RANGE)) + list(range(blocks - RANGE, blocks))
    result = folded(result + gram(rows_one, pair, rows_two, ends))

    def while_sharing():
        for copy in image_edges:
            copy.start()
        packed = low_end() * (1.0 / norm)
        span_gram = tall(
            [lanes(packed, g * span_one, span_one) for g in range(span_one // vecs)])
        prepare(span_gram, 3)
        return span_gram
    packed, span_gram = share(1, all_one_ref, result, span_one + vecs, while_sharing)
    coefs, mixer, table = factor(
        lanes(packed, 0, span_one), lanes(packed, span_one, vecs), span_one, 3)
    small_ref[pl.ds(0, vecs), :] = coefs
    mixer = mixer.astype(BF16)[:, :rows_two]
    for copy in image_edges:
        copy.wait_send()

    def mix_body(chunk, carry):
        out = dot(
            mixer, wide_rows(split_ref, 0, rows_two, [chunk * CHUNK + b for b in range(CHUNK)]), NN)
        value = out[:vecs] + out[vecs:]
        one_ref[:, cols(chunk * CHUNK, CHUNK)] = value
        pieces = chunk_pieces(value)
        for b, piece in enumerate(pieces):
            split_ref[chunk * CHUNK + b, pl.ds(rows_one, pair), :] = split(piece)
        to_major(pieces, block_ref, chunk * CHUNK * vecs, store_major(1, chunk))
        return carry
    lax.fori_loop(0, chunks, mix_body, 0, unroll=2)
    flip_two = flip_copy(1)
    flip_two.start()
    products(1)
    for copy in image_edges + basis_edges:
        copy.wait_recv()
    out = dot(mixer, wide_rows(edge_ref, 0, rows_two, range(2 * RANGE)), NN)
    to_major(chunk_pieces(out[:vecs] + out[vecs:]), near_ref, 0, store_far)
    flip_two.wait_recv()
    flip_products(1)
    gather()
    edge_gather()
    assemble(one_ref, rows_two, 0, blocks)
    result = folded(gram(rows_two, pair, rows_two + pair, range(blocks)))

    def while_sharing_two():
        cross = lanes(table, pair + span_one, span_one)
        cross = cross + jnp.where(lane == row + span_one, 1.0, 0.0)
        low = jnp.concatenate(
            [jnp.zeros((span_one, width), F32), cross,
             jnp.zeros((width - span_two, width), F32)], axis=0)
        prepare(span_gram + low + jnp.where(
            (wide_row < span_one) & (wide_lane >= span_one), low.T, 0.0), 2)
        for copy in vec_edges + basis_edges:
            copy.wait_send()
        flip_one.wait_send()
        flip_two.wait_send()
    packed, _ = share(2, all_two_ref, result, span_two + vecs, while_sharing_two)
    coefs, mixer, _ = factor(
        lanes(packed, 0, span_two), lanes(packed, span_two, vecs), span_two, 2)
    small_ref[pl.ds(vecs, vecs), :] = coefs
    small_ref[pl.ds(pair, pair), :] = mixer


def finish(
    cfg, small_ref, split_ref, one_ref,
    one_hbm, two_hbm, coef_one_hbm, coef_two_hbm,
    two_ref, cut_one_ref, cut_two_ref, store_sem,
):
    _, _, blocks, width, _, _, vecs, kept, _, _ = cfg
    span_one = kept + vecs
    span_two = span_one + vecs
    pieces = 8
    size = blocks // pieces * width
    stores = [pltpu.make_async_copy(one_ref, one_hbm.at[0], store_sem.at[0])]
    stores[-1].start()
    mixer = small_ref[pl.ds(2 * vecs, 2 * vecs), :].astype(BF16)[:, :2 * (span_two + vecs)]
    for piece in range(pieces):
        part = pl.ds(piece * size, size)
        tiles = range(piece * (blocks // pieces), (piece + 1) * (blocks // pieces))
        out = dot(mixer, jnp.concatenate([split_ref[tile] for tile in tiles], axis=1), NN)
        two_ref[:, part] = out[:vecs] + out[vecs:]
        stores.append(pltpu.make_async_copy(
            two_ref.at[:, part], two_hbm.at[0, :, part], store_sem.at[1 + piece]))
        stores[-1].start()
    cut_one_ref[...] = small_ref[pl.ds(0, vecs), :span_one + vecs]
    cut_two_ref[...] = small_ref[pl.ds(vecs, vecs), :span_two + vecs]
    stores.append(pltpu.make_async_copy(cut_one_ref, coef_one_hbm, store_sem.at[1 + pieces]))
    stores.append(pltpu.make_async_copy(cut_two_ref, coef_two_hbm, store_sem.at[2 + pieces]))
    for copy in stores[-2:]:
        copy.start()
    for copy in stores:
        copy.wait()


def per_device(
    vectors, basis, potential, hop_table, soc_table, nbr_block, nbr_type, nbr_count, flip_block
):
    blocks, slots = nbr_block.shape
    types, width, _ = hop_table.shape
    vecs, kept = vectors.shape[1], basis.shape[1]
    dom_total = lax.axis_size("dom")
    group_doms = 4 if dom_total % 4 == 0 else 1
    groups = dom_total // group_doms
    norm = float(2 * blocks * width * dom_total)
    direct = dom_total <= 32
    cfg = (dom_total, group_doms, blocks, width, types, slots, vecs, kept, norm, direct)
    count = blocks * width
    pair = 2 * vecs
    span_one, span_two = kept + vecs, kept + 2 * vecs
    kinds = types + 1
    seats = 2 * dom_total if direct else 1
    row_count = lambda size: -(-vecs // (width // size))
    vmem = pl.BlockSpec(memory_space=pltpu.VMEM)
    hbm = pl.BlockSpec(memory_space=pltpu.HBM)
    dma = pltpu.SemaphoreType.DMA
    shape = jax.ShapeDtypeStruct
    one, parts, small = pl.pallas_call(
        functools.partial(kernel, cfg),
        name="krylov",
        out_shape=(
            pltpu.VMEM((vecs, count), F32),
            pltpu.VMEM((blocks, 2 * (span_two + vecs), width), BF16),
            pltpu.VMEM((4 * vecs, width), F32),
        ),
        in_specs=[hbm] * 9,
        out_specs=(vmem, vmem, vmem),
        scratch_shapes=[
            pltpu.VMEM((vecs, count), F32),
            pltpu.VMEM((kept, count), F32),
            pltpu.VMEM((1, count), F32),
            pltpu.VMEM((types * width, width), BF16),
            pltpu.VMEM(soc_table.shape, BF16),
            pltpu.VMEM((slots, blocks), I32),
            pltpu.VMEM((slots, blocks), I32),
            pltpu.VMEM((1, blocks), I32),
            pltpu.VMEM((1, blocks), I32),
            pltpu.VMEM((blocks * vecs, width), F32),
            pltpu.VMEM((2 * RANGE, 2 * span_two, width), BF16),
            pltpu.VMEM((2, vecs, blocks, width), BF16),
            pltpu.VMEM((2, vecs, blocks, width), BF16),
            pltpu.VMEM((2 * RANGE * vecs, width), F32),
            pltpu.VMEM((vecs, 2 * RANGE, width), BF16),
            pltpu.VMEM((vecs, 2 * kinds * blocks, width), BF16),
            pltpu.VMEM((vecs, 4 * RANGE * types, width), BF16),
            pltpu.VMEM((kinds, blocks, width), BF16),
            pltpu.VMEM((2 * RANGE, 2 * RANGE * types), BF16),
            pltpu.VMEM((vecs, width), F32),
            pltpu.VMEM((3, width, 2 * width), BF16),
            pltpu.VMEM((3, 2 * group_doms, vecs, width), F32),
            pltpu.VMEM((3, groups, vecs, width), F32),
            pltpu.VMEM((seats, vecs, width), F32),
            pltpu.VMEM((seats, row_count(span_one + vecs), width), F32),
            pltpu.VMEM((seats, row_count(span_two + vecs), width), F32),
            dma((9,)),
            dma((2,)), dma((2,)),
            dma((3, 2)), dma((3, 2)),
            dma((3, 2 * group_doms)), dma((3, 2 * group_doms)),
            dma((3, groups)), dma((3, groups)),
            dma((3,)), dma((3,)),
        ],
        compiler_params=pltpu.CompilerParams(
            collective_id=0, has_side_effects=True, vmem_limit_bytes=32 * 1024 * 1024),
    )(*[pltpu.with_memory_space_constraint(value, pltpu.HBM) for value in (
        vectors, basis, potential, hop_table.reshape(types * width, width), soc_table,
        nbr_block.T, nbr_type.T, nbr_count.reshape(1, blocks), flip_block.reshape(1, blocks))])
    one, two, coef_one, coef_two = pl.pallas_call(
        functools.partial(finish, cfg),
        name="finish",
        out_shape=(
            shape((1, vecs, count), F32),
            shape((1, vecs, count), F32),
            shape((vecs, span_one + vecs), F32),
            shape((vecs, span_two + vecs), F32),
        ),
        in_specs=[vmem, vmem, vmem],
        out_specs=(hbm,) * 4,
        scratch_shapes=[
            pltpu.VMEM((vecs, count), F32),
            pltpu.VMEM((vecs, span_one + vecs), F32),
            pltpu.VMEM((vecs, span_two + vecs), F32),
            dma((11,)),
        ],
        compiler_params=pltpu.CompilerParams(vmem_limit_bytes=16 * 1024 * 1024),
    )(small, parts, one)
    return one, two, coef_one.T, coef_two.T


def solution(mesh):
    return jax.shard_map(
        per_device,
        mesh=mesh,
        in_specs=(
            P("spin", None, "dom"),
            P("spin", None, "dom"),
            P("spin", "dom"),
            P(),
            P(),
            P("dom", None),
            P("dom", None),
            P("dom"),
            P("dom"),
        ),
        out_specs=(P("spin", None, "dom"), P("spin", None, "dom"), P(), P()),
        check_vma=False,
    )
```

```python
import functools
import jax
import jax.numpy as jnp
from jax import lax
from jax.experimental import pallas as pl
from jax.experimental.pallas import tpu as pltpu
from jax.sharding import PartitionSpec as P

RANGE = 8
STRIDE = 32
CHUNK = 16
MESH = pl.DeviceIdType.MESH
NT = (((1,), (1,)), ((), ()))
NN = (((1,), (0,)), ((), ()))
F32, BF16, I32 = jnp.float32, jnp.bfloat16, jnp.int32


def high_dot(left, right, dims):
    return lax.dot_general(
        left, right, dims, precision=lax.Precision.HIGHEST, preferred_element_type=F32
    )


def dot(left, right, dims):
    return lax.dot_general(left, right, dims, preferred_element_type=F32)


def split(value):
    low = value - value.astype(BF16).astype(F32)
    return jnp.concatenate([value, low], axis=0).astype(BF16)


def halves(value):
    high = value.astype(BF16)
    return high, (value - high.astype(F32)).astype(BF16)


def kernel(
    cfg,
    vec_hbm, basis_hbm, pot_hbm, hop_hbm, soc_hbm, nbr_hbm, type_hbm, count_hbm, flip_hbm,
    one_ref, split_ref, small_ref,
    vec_ref, basis_ref, pot_ref, hop_ref, soc_ref, nbr_ref, type_ref, count_ref, fliploc_ref,
    block_ref, edge_ref, major_ref, other_ref, near_ref, far_ref, prod_ref, edge_prod_ref,
    select_ref, edge_select_ref, fold_ref, inner_ref, weight_ref, stage_a_ref, stage_b_ref,
    all_low_ref, all_one_ref, all_two_ref,
    load_sem, flip_send, flip_recv, edge_send, edge_recv, a_send, a_recv, b_send, b_recv,
    all_send, all_recv,
):
    dom_total, group_doms, blocks, width, types, slots, vecs, kept, norm, direct = cfg
    pair = 2 * vecs
    kept_groups = kept // vecs
    span_one = kept + vecs
    span_two = span_one + vecs
    rows_one = 2 * span_one
    rows_two = 2 * span_two
    kinds = types + 1
    devices = 2 * dom_total

    sources = [
        (vec_hbm.at[0], vec_ref), (nbr_hbm, nbr_ref), (type_hbm, type_ref),
        (count_hbm, count_ref), (flip_hbm, fliploc_ref), (basis_hbm.at[0], basis_ref),
        (hop_hbm, hop_ref), (soc_hbm, soc_ref), (pot_hbm, pot_ref)]
    loads = [
        pltpu.make_async_copy(src, dst, load_sem.at[n]) for n, (src, dst) in enumerate(sources)]
    for copy in loads:
        copy.start()
    groups = dom_total // group_doms
    group_size = 2 * group_doms
    dom, spin = lax.axis_index("dom"), lax.axis_index("spin")
    rank_a = (dom % group_doms) * 2 + spin
    rank_b = dom // group_doms
    dom_base = rank_b * group_doms
    left, right = (dom + dom_total - 1) % dom_total, (dom + 1) % dom_total

    def peer_a(shift):
        other = (rank_a + shift) % group_size
        return (dom_base + other // 2, other % 2)

    def peer_b(shift):
        return (((rank_b + shift) % groups) * group_doms + dom % group_doms, spin)

    far_first = sorted(range(dom_total), key=lambda shift: -min(shift, dom_total - shift))

    def everyone():
        for shift in far_first:
            ahead = dom + shift
            target = jnp.where(ahead >= dom_total, ahead - dom_total, ahead)
            if shift:
                yield (target, spin)
            yield (target, 1 - spin)

    barrier = pltpu.get_barrier_semaphore()
    if direct:
        greeted = list(everyone())
    else:
        greeted = [peer_a(shift) for shift in range(1, group_size)]
        greeted += [peer_b(shift) for shift in range(1, groups)]
        greeted += [(left, spin), (right, spin)]
    for target in greeted:
        pl.semaphore_signal(barrier, inc=1, device_id=target, device_id_type=MESH)

    lane = lax.broadcasted_iota(I32, (vecs, width), 1)
    row = lax.broadcasted_iota(I32, (vecs, width), 0)

    def cols(tile, size=1):
        return pl.ds(pl.multiple_of(tile * width, width), size * width)

    def flip_copy(app):
        return pltpu.make_async_remote_copy(
            src_ref=major_ref.at[app], dst_ref=other_ref.at[app],
            send_sem=flip_send.at[app], recv_sem=flip_recv.at[app],
            device_id=(dom, 1 - spin), device_id_type=MESH)

    def edge_copies(n, first, rows):
        part = pl.ds(first, rows)
        tail = pltpu.make_async_remote_copy(
            src_ref=split_ref.at[pl.ds(blocks - RANGE, RANGE), part],
            dst_ref=edge_ref.at[pl.ds(0, RANGE), part],
            send_sem=edge_send.at[n, 0], recv_sem=edge_recv.at[n, 0],
            device_id=(right, spin), device_id_type=MESH)
        head = pltpu.make_async_remote_copy(
            src_ref=split_ref.at[pl.ds(0, RANGE), part],
            dst_ref=edge_ref.at[pl.ds(RANGE, RANGE), part],
            send_sem=edge_send.at[n, 1], recv_sem=edge_recv.at[n, 1],
            device_id=(left, spin), device_id_type=MESH)
        return tail, head

    def to_major(value, scratch, base, store):
        for b, piece in enumerate(value):
            scratch[pl.ds(base + b * vecs, vecs), :] = piece
        for k in range(vecs):
            store(k, scratch[pl.ds(base + k, CHUNK, stride=vecs), :].astype(BF16))

    def tree(parts):
        while len(parts) > 1:
            parts = [sum(parts[p + 1:p + 2], parts[p]) for p in range(0, len(parts), 2)]
        return parts[0]

    def stage(n, ref, send, recv, rank, size, peer):
        def copy(shift, slot):
            return pltpu.make_async_remote_copy(
                src_ref=ref.at[n, rank], dst_ref=ref.at[n, slot],
                send_sem=send.at[n, shift], recv_sem=recv.at[n, slot],
                device_id=peer(shift), device_id_type=MESH)

        def begin(value):
            ref[n, rank] = value
            for shift in range(1, size):
                copy(shift, rank).start()

        def end():
            for shift in range(1, size):
                copy(shift, (rank + size - shift) % size).wait_recv()
            for shift in range(1, size):
                copy(shift, rank).wait_send()
            return tree([ref[n, slot] for slot in range(size)])
        return begin, end

    def staged(n):
        begin_a, end_a = stage(n, stage_a_ref, a_send, a_recv, rank_a, group_size, peer_a)
        begin_b, end_b = stage(n, stage_b_ref, b_send, b_recv, rank_b, groups, peer_b)
        return begin_a, lambda: begin_b(end_a()), end_b

    def exchange(n, ref):
        if not direct:
            return staged(n)
        me = dom * 2 + spin

        def begin(value):
            ref[me] = value
            for target in everyone():
                pltpu.make_async_remote_copy(
                    src_ref=ref.at[me], dst_ref=ref.at[me],
                    send_sem=all_send.at[n], recv_sem=all_recv.at[n],
                    device_id=target, device_id_type=MESH).start()

        def end():
            others = ref.at[pl.ds(0, devices - 1)]
            whole = pltpu.make_async_remote_copy(
                src_ref=others, dst_ref=others, send_sem=all_send.at[n], recv_sem=all_recv.at[n],
                device_id=(dom, 1 - spin), device_id_type=MESH)
            whole.wait_recv()
            whole.wait_send()
            return tree([ref[slot] for slot in range(devices)])
        return begin, lambda: None, end

    def share(n, ref, value, size, work):
        begin, middle, end = exchange(n, ref)
        if not direct:
            begin(value)
            done = work()
            middle()
            return end() * (1.0 / norm), done
        per = width // size
        rows = -(-vecs // per)
        out = value
        for q in range(1, per):
            moved = pltpu.roll(pltpu.roll(value, (-q * rows) % vecs, 0), q * size, 1)
            out = jnp.where((lane >= q * size) & (lane < (q + 1) * size), moved, out)
        begin(out[:rows])
        done = work()
        fold_ref[pl.ds(0, rows), :] = end()
        total = fold_ref[...] * (1.0 / norm)
        out = jnp.where((lane < size) & (row < rows), total, 0.0)
        for q in range(1, per):
            moved = pltpu.roll(pltpu.roll(total, (q * rows) % vecs, 0), width - q * size, 1)
            out = jnp.where((lane < size) & (row >= q * rows) & (row < (q + 1) * rows), moved, out)
        return out, done

    def lanes(value, start, size):
        moved = value if start == 0 else pltpu.roll(value, width - start, 1)
        return jnp.where(lane < size, moved, 0.0)

    def tall(pieces):
        pad = width - vecs * len(pieces)
        return jnp.concatenate(list(pieces) + [jnp.zeros((pad, width), F32)], axis=0)

    def folded(value):
        wide = value.shape[1]
        fold_ref[:, pl.ds(0, wide)] = value[:vecs] + value[vecs:]
        both = fold_ref[...]
        both = both + pltpu.roll(both, width - vecs, 1)
        out = jnp.where(lane < vecs, both, 0.0)
        for g in range(1, wide // pair):
            inside = (lane >= vecs * g) & (lane < vecs * (g + 1))
            out = jnp.where(inside, pltpu.roll(both, width - vecs * g, 1), out)
        return out

    def wide_rows(ref, first, rows, tiles):
        return jnp.concatenate([ref[tile, pl.ds(first, rows), :] for tile in tiles], axis=1)

    def gram(first, rows, size, tiles):
        tiles = list(tiles)
        middle = len(tiles) // 2
        return sum(
            dot(wide_rows(split_ref, first, rows, part), wide_rows(split_ref, 0, size, part), NT)
            for part in (tiles[:middle], tiles[middle:]))

    def prepare(span_gram, count):
        eye = jnp.where(wide_row == wide_lane, 1.0, 0.0)
        once = 2.0 * eye - span_gram
        left_over = high_dot(eye - span_gram, eye - span_gram, NN)
        square = once + high_dot(left_over, once, NN)
        for n, table in enumerate([once, square, left_over][:count]):
            high, low = halves(table)
            weight_ref[n, :, pl.ds(0, width)] = high
            weight_ref[n, :, pl.ds(width, width)] = low

    def factor(first_t, image_gram, span_count, count):
        first = split(first_t)
        mixed = []
        for n in range(count):
            out = dot(first, weight_ref[n], NN)
            out = out[:vecs] + out[vecs:]
            mixed.append(out[:, :width] + out[:, width:])
        total_t = mixed[0]
        out = dot(split(mixed[1]), first, NT)
        fold_ref[:, pl.ds(0, pair)] = out[:vecs] + out[vecs:]
        both = fold_ref[...]
        square = image_gram - both - pltpu.roll(both, width - vecs, 1)
        table = jnp.where(lane < vecs, square, jnp.where(lane == row + vecs, 1.0, 0.0))
        table = table - pltpu.roll(total_t, pair, 1)
        if count > 2:
            table = table + pltpu.roll(mixed[2], pair + span_count, 1)
        lower = jnp.zeros((vecs, width), F32)
        for j in range(vecs):
            column = jnp.broadcast_to(table[:, j:j + 1], (vecs, width))
            pivot_row = jnp.broadcast_to(table[j:j + 1, :], (vecs, width))
            pivot = jnp.broadcast_to(column[j:j + 1, :], (vecs, width))
            scale = lax.rsqrt(pivot)
            column = column * scale
            lower = jnp.where((lane == j) & (row >= j), column, lower)
            pivot_row = pivot_row * scale
            table = jnp.where(
                row == j, pivot_row, jnp.where(row > j, table - column * pivot_row, table))
        mixer = jnp.zeros((vecs, width), F32)
        for g in range(span_count // vecs + 1):
            source = pair + vecs * g if g < span_count // vecs else vecs
            moved = pltpu.roll(table, (pair * g - source) % width, 1)
            mixer = jnp.where((lane >= pair * g) & (lane < pair * g + vecs), moved, mixer)
        mixer = mixer + pltpu.roll(mixer, vecs, 1)
        low = mixer - mixer.astype(BF16).astype(F32)
        return (
            total_t + pltpu.roll(lower, span_count, 1), jnp.concatenate([mixer, low], axis=0), table)

    def split_products(out, k, base, half_size, size, ref):
        high, low = halves(out)
        ref[k, pl.ds(base, size), :] = high
        ref[k, pl.ds(half_size + base, size), :] = low

    def products(app):
        def body(two, carry):
            weights = hop_ref[pl.ds(pl.multiple_of(two * 2 * width, 2 * width), 2 * width), :]
            for k in range(vecs):
                out = dot(major_ref[app, k], weights, NT)
                for half in range(2):
                    at = pl.multiple_of((two * 2 + half) * blocks, blocks)
                    split_products(
                        out[:, half * width:(half + 1) * width], k, at, kinds * blocks, blocks,
                        prod_ref)
            return carry
        lax.fori_loop(0, types // 2, body, 0, unroll=2)

    def flip_products(app):
        for k in range(vecs):
            out = dot(other_ref[app, k], soc_ref[spin], NT)
            split_products(out, k, types * blocks, kinds * blocks, blocks, prod_ref)

    def gather():
        def body(two, carry):
            chosen = jnp.concatenate([select_ref[n % kinds] for n in range(2 * kinds)], axis=1)
            held = jnp.concatenate([prod_ref[2 * two], prod_ref[2 * two + 1]], axis=1)
            out = dot(chosen, held, NN)
            for half in range(2):
                for i in range(blocks // vecs):
                    block_ref[pl.ds(i * vecs * vecs + 2 * two + half, vecs, stride=vecs), :] = (
                        out[i * vecs:(i + 1) * vecs, half * width:(half + 1) * width])
            return carry
        lax.fori_loop(0, vecs // 2, body, 0, unroll=2)

    def edge_gather():
        reach = 2 * RANGE
        source = far_ref[...].reshape(vecs * reach, width)

        for two in range(types // 2):
            out = dot(source, hop_ref[pl.ds(two * 2 * width, 2 * width), :], NT)
            for half in range(2):
                for k in range(vecs):
                    split_products(
                        out[k * reach:(k + 1) * reach, half * width:(half + 1) * width], k,
                        (two * 2 + half) * reach, types * reach, reach, edge_prod_ref)
        chosen = jnp.concatenate([edge_select_ref[...]] * 2, axis=1)
        for two in range(vecs // 2):
            held = jnp.concatenate([edge_prod_ref[2 * two], edge_prod_ref[2 * two + 1]], axis=1)
            out = dot(chosen, held, NN)
            for half in range(2):
                for end, base in enumerate((0, (blocks - RANGE) * vecs)):
                    at = pl.ds(base + 2 * two + half, RANGE, stride=vecs)
                    block_ref[at, :] = block_ref[at, :] + out[
                        end * RANGE:(end + 1) * RANGE, half * width:(half + 1) * width]

    def assemble(field_ref, first, low, high):
        def body(block, carry):
            image = pot_ref[pl.ds(0, 1), cols(block)] * field_ref[:, cols(block)]
            at = pl.multiple_of(block * vecs, vecs)
            image = image + block_ref[pl.ds(at, vecs), :]
            split_ref[block, pl.ds(first, pair), :] = split(image)
            return carry
        lax.fori_loop(low, high, body, 0, unroll=8)

    def chunk_pieces(value):
        return [value[:, b * width:(b + 1) * width] for b in range(CHUNK)]

    def store_major(app, chunk):
        def store(k, rounded):
            major_ref[app, k, pl.ds(pl.multiple_of(chunk * CHUNK, CHUNK), CHUNK), :] = rounded
        return store

    def round_body(chunk, carry):
        pieces = chunk_pieces(vec_ref[:, cols(chunk * CHUNK, CHUNK)])
        for b, piece in enumerate(pieces):
            split_ref[chunk * CHUNK + b, pl.ds(2 * kept, pair), :] = split(piece)
        to_major(pieces, block_ref, chunk * CHUNK * vecs, store_major(0, chunk))
        return carry

    def store_far(k, rounded):
        far_ref[k] = rounded

    wide_row = lax.broadcasted_iota(I32, (width, width), 0)
    wide_lane = lax.broadcasted_iota(I32, (width, width), 1)
    chunks = blocks // CHUNK
    loads[0].wait()
    round_body(0, 0)
    round_body(chunks - 1, 0)
    pl.semaphore_wait(barrier, len(greeted))
    vec_edges = edge_copies(0, 2 * kept, pair)
    for copy in vec_edges:
        copy.start()
    lax.fori_loop(1, chunks - 1, round_body, 0)
    flip_one = flip_copy(0)
    flip_one.start()
    for copy in loads[1:5]:
        copy.wait()

    local = lax.broadcasted_iota(I32, (slots, blocks), 1)
    slot_at = lax.broadcasted_iota(I32, (slots, blocks), 0)
    shift = nbr_ref[...] - (dom * blocks + local) + RANGE
    total = dom_total * blocks
    shift = jnp.where(shift < 0, shift + total, shift)
    shift = jnp.where(shift >= total, shift - total, shift)
    place = local + shift - RANGE
    live = slot_at < count_ref[...]
    inside = (place >= 0) & (place < blocks)
    code = jnp.where(live & inside, type_ref[...] * STRIDE + shift, -1)
    edge_code = jnp.where(place < 0, place + RANGE, place - blocks + RANGE)
    edge_code = jnp.where(live & ~inside, type_ref[...] * (2 * RANGE) + edge_code, -1)

    def counts(codes, base):
        wanted = row + base
        return tree([jnp.where(codes[s:s + 1, :] == wanted, 1.0, 0.0) for s in range(slots)])

    band = (wide_lane - wide_row <= RANGE) & (wide_row - wide_lane <= RANGE)
    per_tile = width // STRIDE
    blank = jnp.zeros((vecs, width), F32)
    for tile in range(types // per_tile):
        pieces = []
        for r in range(width // vecs):
            live_rows = (r * vecs) % STRIDE <= 2 * RANGE
            pieces.append(counts(code, tile * width + r * vecs) if live_rows else blank)
        table = jnp.concatenate(pieces, axis=0).T
        for t in range(per_tile):
            moved = pltpu.roll(
                table, (-RANGE - STRIDE * t) % width, 1, stride=1, stride_axis=0)
            select_ref[tile * per_tile + t] = jnp.where(band, moved, 0.0).astype(BF16)
    flip_local = fliploc_ref[...] - dom * blocks
    select_ref[types] = jnp.where(flip_local == wide_row, 1.0, 0.0).T.astype(BF16)
    table = jnp.concatenate(
        [counts(edge_code, r * vecs) for r in range(width // vecs)], axis=0).T
    edge_select_ref[...] = jnp.concatenate(
        [table[:RANGE], table[blocks - RANGE:]], axis=0).astype(BF16)
    fold_ref[...] = jnp.zeros((vecs, width), F32)

    loads[5].wait()

    def split_basis(chunk, carry):
        for b in range(4):
            block = chunk * 4 + b
            for g in range(kept_groups):
                split_ref[block, pl.ds(g * pair, pair), :] = split(
                    basis_ref[pl.ds(g * vecs, vecs), cols(block)])
        return carry
    lax.fori_loop(0, blocks // 4, split_basis, 0, unroll=2)
    basis_edges = edge_copies(1, 0, 2 * kept)
    for copy in basis_edges:
        copy.start()
    low_gram = gram(0, rows_one, rows_one, range(blocks))
    packed_low = jnp.zeros((vecs, width), F32)
    for g in range(span_one // vecs):
        piece = folded(low_gram[g * pair:(g + 1) * pair])
        packed_low = packed_low + (pltpu.roll(piece, g * span_one, 1) if g else piece)
    low_begin, low_middle, low_end = exchange(0, all_low_ref)
    low_begin(packed_low)
    for copy in loads[6:]:
        copy.wait()

    products(0)
    low_middle()
    flip_one.wait_recv()
    flip_products(0)
    gather()
    assemble(vec_ref, rows_one, RANGE, blocks - RANGE)
    inner_ref[...] = gram(rows_one, pair, rows_two, range(RANGE, blocks - RANGE))
    for copy in vec_edges:
        copy.wait_recv()
    to_major(
        [edge_ref[b, pl.ds(2 * kept, pair), :].astype(F32)[:vecs] for b in range(2 * RANGE)],
        near_ref, 0, store_far)
    edge_gather()
    assemble(vec_ref, rows_one, 0, RANGE)
    assemble(vec_ref, rows_one, blocks - RANGE, blocks)
    image_edges = edge_copies(2, rows_one, pair)
    ends = list(range(RANGE)) + list(range(blocks - RANGE, blocks))
    result = folded(inner_ref[...] + gram(rows_one, pair, rows_two, ends))

    def while_sharing():
        for copy in image_edges:
            copy.start()
        packed = low_end() * (1.0 / norm)
        span_gram = tall(
            [lanes(packed, g * span_one, span_one) for g in range(span_one // vecs)])
        prepare(span_gram, 3)
        return span_gram
    packed, span_gram = share(1, all_one_ref, result, span_one + vecs, while_sharing)
    coefs, mixer, table = factor(
        lanes(packed, 0, span_one), lanes(packed, span_one, vecs), span_one, 3)
    small_ref[pl.ds(0, vecs), :] = coefs
    mixer = mixer.astype(BF16)[:, :rows_two]
    for copy in image_edges:
        copy.wait_send()

    def mix_body(chunk, carry):
        out = dot(
            mixer, wide_rows(split_ref, 0, rows_two, [chunk * CHUNK + b for b in range(CHUNK)]), NN)
        value = out[:vecs] + out[vecs:]
        one_ref[:, cols(chunk * CHUNK, CHUNK)] = value
        pieces = chunk_pieces(value)
        for b, piece in enumerate(pieces):
            split_ref[chunk * CHUNK + b, pl.ds(rows_one, pair), :] = split(piece)
        to_major(pieces, block_ref, chunk * CHUNK * vecs, store_major(1, chunk))
        return carry
    lax.fori_loop(0, chunks, mix_body, 0, unroll=2)
    flip_two = flip_copy(1)
    flip_two.start()
    products(1)
    for copy in image_edges + basis_edges:
        copy.wait_recv()
    out = dot(mixer, wide_rows(edge_ref, 0, rows_two, range(2 * RANGE)), NN)
    to_major(chunk_pieces(out[:vecs] + out[vecs:]), near_ref, 0, store_far)
    flip_two.wait_recv()
    flip_products(1)
    gather()
    edge_gather()
    assemble(one_ref, rows_two, 0, blocks)
    result = folded(gram(rows_two, pair, rows_two + pair, range(blocks)))

    def while_sharing_two():
        cross = lanes(table, pair + span_one, span_one)
        cross = cross + jnp.where(lane == row + span_one, 1.0, 0.0)
        low = jnp.concatenate(
            [jnp.zeros((span_one, width), F32), cross,
             jnp.zeros((width - span_two, width), F32)], axis=0)
        prepare(span_gram + low + jnp.where(
            (wide_row < span_one) & (wide_lane >= span_one), low.T, 0.0), 2)
        for copy in vec_edges + basis_edges:
            copy.wait_send()
        flip_one.wait_send()
        flip_two.wait_send()
    packed, _ = share(2, all_two_ref, result, span_two + vecs, while_sharing_two)
    coefs, mixer, _ = factor(
        lanes(packed, 0, span_two), lanes(packed, span_two, vecs), span_two, 2)
    small_ref[pl.ds(vecs, vecs), :] = coefs
    small_ref[pl.ds(pair, pair), :] = mixer


def finish(
    cfg, small_ref, split_ref, one_ref,
    one_hbm, two_hbm, coef_one_hbm, coef_two_hbm,
    two_ref, cut_one_ref, cut_two_ref, store_sem,
):
    _, _, blocks, width, _, _, vecs, kept, _, _ = cfg
    span_one = kept + vecs
    span_two = span_one + vecs
    pieces = 8
    size = blocks // pieces * width
    stores = [pltpu.make_async_copy(one_ref, one_hbm.at[0], store_sem.at[0])]
    stores[-1].start()
    mixer = small_ref[pl.ds(2 * vecs, 2 * vecs), :].astype(BF16)[:, :2 * (span_two + vecs)]
    for piece in range(pieces):
        part = pl.ds(piece * size, size)
        tiles = range(piece * (blocks // pieces), (piece + 1) * (blocks // pieces))
        out = dot(mixer, jnp.concatenate([split_ref[tile] for tile in tiles], axis=1), NN)
        two_ref[:, part] = out[:vecs] + out[vecs:]
        stores.append(pltpu.make_async_copy(
            two_ref.at[:, part], two_hbm.at[0, :, part], store_sem.at[1 + piece]))
        stores[-1].start()
    cut_one_ref[...] = small_ref[pl.ds(0, vecs), :span_one + vecs]
    cut_two_ref[...] = small_ref[pl.ds(vecs, vecs), :span_two + vecs]
    stores.append(pltpu.make_async_copy(cut_one_ref, coef_one_hbm, store_sem.at[1 + pieces]))
    stores.append(pltpu.make_async_copy(cut_two_ref, coef_two_hbm, store_sem.at[2 + pieces]))
    for copy in stores[-2:]:
        copy.start()
    for copy in stores:
        copy.wait()


def per_device(
    vectors, basis, potential, hop_table, soc_table, nbr_block, nbr_type, nbr_count, flip_block
):
    blocks, slots = nbr_block.shape
    types, width, _ = hop_table.shape
    vecs, kept = vectors.shape[1], basis.shape[1]
    dom_total = lax.axis_size("dom")
    group_doms = 4 if dom_total % 4 == 0 else 1
    groups = dom_total // group_doms
    norm = float(2 * blocks * width * dom_total)
    direct = dom_total <= 32
    cfg = (dom_total, group_doms, blocks, width, types, slots, vecs, kept, norm, direct)
    count = blocks * width
    pair = 2 * vecs
    span_one, span_two = kept + vecs, kept + 2 * vecs
    kinds = types + 1
    seats = 2 * dom_total if direct else 1
    rounds, near, far = (1, 1, 1) if direct else (3, 2 * group_doms, groups)
    row_count = lambda size: -(-vecs // (width // size))
    vmem = pl.BlockSpec(memory_space=pltpu.VMEM)
    hbm = pl.BlockSpec(memory_space=pltpu.HBM)
    dma = pltpu.SemaphoreType.DMA
    shape = jax.ShapeDtypeStruct
    one, parts, small = pl.pallas_call(
        functools.partial(kernel, cfg),
        name="krylov",
        out_shape=(
            pltpu.VMEM((vecs, count), F32),
            pltpu.VMEM((blocks, 2 * (span_two + vecs), width), BF16),
            pltpu.VMEM((4 * vecs, width), F32),
        ),
        in_specs=[hbm] * 9,
        out_specs=(vmem, vmem, vmem),
        scratch_shapes=[
            pltpu.VMEM((vecs, count), F32),
            pltpu.VMEM((kept, count), F32),
            pltpu.VMEM((1, count), F32),
            pltpu.VMEM((types * width, width), BF16),
            pltpu.VMEM(soc_table.shape, BF16),
            pltpu.VMEM((slots, blocks), I32),
            pltpu.VMEM((slots, blocks), I32),
            pltpu.VMEM((1, blocks), I32),
            pltpu.VMEM((1, blocks), I32),
            pltpu.VMEM((blocks * vecs, width), F32),
            pltpu.VMEM((2 * RANGE, 2 * span_two, width), BF16),
            pltpu.VMEM((2, vecs, blocks, width), BF16),
            pltpu.VMEM((2, vecs, blocks, width), BF16),
            pltpu.VMEM((2 * RANGE * vecs, width), F32),
            pltpu.VMEM((vecs, 2 * RANGE, width), BF16),
            pltpu.VMEM((vecs, 2 * kinds * blocks, width), BF16),
            pltpu.VMEM((vecs, 4 * RANGE * types, width), BF16),
            pltpu.VMEM((kinds, blocks, width), BF16),
            pltpu.VMEM((2 * RANGE, 2 * RANGE * types), BF16),
            pltpu.VMEM((vecs, width), F32),
            pltpu.VMEM((pair, 2 * span_two), F32),
            pltpu.VMEM((3, width, 2 * width), BF16),
            pltpu.VMEM((rounds, near, vecs, width), F32),
            pltpu.VMEM((rounds, far, vecs, width), F32),
            pltpu.VMEM((seats, vecs, width), F32),
            pltpu.VMEM((seats, row_count(span_one + vecs), width), F32),
            pltpu.VMEM((seats, row_count(span_two + vecs), width), F32),
            dma((9,)),
            dma((2,)), dma((2,)),
            dma((3, 2)), dma((3, 2)),
            dma((rounds, near)), dma((rounds, near)),
            dma((rounds, far)), dma((rounds, far)),
            dma((3,)), dma((3,)),
        ],
        compiler_params=pltpu.CompilerParams(
            collective_id=0, has_side_effects=True, vmem_limit_bytes=32 * 1024 * 1024),
    )(*[pltpu.with_memory_space_constraint(value, pltpu.HBM) for value in (
        vectors, basis, potential, hop_table.reshape(types * width, width), soc_table,
        nbr_block.T, nbr_type.T, nbr_count.reshape(1, blocks), flip_block.reshape(1, blocks))])
    one, two, coef_one, coef_two = pl.pallas_call(
        functools.partial(finish, cfg),
        name="finish",
        out_shape=(
            shape((1, vecs, count), F32),
            shape((1, vecs, count), F32),
            shape((vecs, span_one + vecs), F32),
            shape((vecs, span_two + vecs), F32),
        ),
        in_specs=[vmem, vmem, vmem],
        out_specs=(hbm,) * 4,
        scratch_shapes=[
            pltpu.VMEM((vecs, count), F32),
            pltpu.VMEM((vecs, span_one + vecs), F32),
            pltpu.VMEM((vecs, span_two + vecs), F32),
            dma((11,)),
        ],
        compiler_params=pltpu.CompilerParams(vmem_limit_bytes=16 * 1024 * 1024),
    )(small, parts, one)
    return one, two, coef_one.T, coef_two.T


def solution(mesh):
    return jax.shard_map(
        per_device,
        mesh=mesh,
        in_specs=(
            P("spin", None, "dom"),
            P("spin", None, "dom"),
            P("spin", "dom"),
            P(),
            P(),
            P("dom", None),
            P("dom", None),
            P("dom"),
            P("dom"),
        ),
        out_specs=(P("spin", None, "dom"), P("spin", None, "dom"), P(), P()),
        check_vma=False,
    )
```

```python
import functools
import jax
import jax.numpy as jnp
from jax import lax
from jax.experimental import pallas as pl
from jax.experimental.pallas import tpu as pltpu
from jax.sharding import PartitionSpec as P

RANGE = 8
STRIDE = 32
CHUNK = 16
MESH = pl.DeviceIdType.MESH
NT = (((1,), (1,)), ((), ()))
NN = (((1,), (0,)), ((), ()))
F32, BF16, I32 = jnp.float32, jnp.bfloat16, jnp.int32


def high_dot(left, right, dims):
    return lax.dot_general(
        left, right, dims, precision=lax.Precision.HIGHEST, preferred_element_type=F32
    )


def dot(left, right, dims):
    return lax.dot_general(left, right, dims, preferred_element_type=F32)


def split(value):
    low = value - value.astype(BF16).astype(F32)
    return jnp.concatenate([value, low], axis=0).astype(BF16)


def halves(value):
    high = value.astype(BF16)
    return high, (value - high.astype(F32)).astype(BF16)


def kernel(
    cfg,
    vec_hbm, basis_hbm, pot_hbm, hop_hbm, soc_hbm, nbr_hbm, type_hbm, count_hbm, flip_hbm,
    one_ref, split_ref, small_ref,
    vec_ref, basis_ref, pot_ref, hop_ref, soc_ref, nbr_ref, type_ref, count_ref, fliploc_ref,
    block_ref, edge_ref, major_ref, other_ref, near_ref, far_ref, prod_ref, edge_prod_ref,
    select_ref, edge_select_ref, fold_ref, inner_ref, weight_ref, stage_a_ref, stage_b_ref,
    all_low_ref, all_one_ref, all_two_ref,
    load_sem, flip_send, flip_recv, edge_send, edge_recv, a_send, a_recv, b_send, b_recv,
    all_send, all_recv,
):
    dom_total, group_doms, blocks, width, types, slots, vecs, kept, norm, direct = cfg
    pair = 2 * vecs
    kept_groups = kept // vecs
    span_one = kept + vecs
    span_two = span_one + vecs
    rows_one = 2 * span_one
    rows_two = 2 * span_two
    kinds = types + 1
    devices = 2 * dom_total

    sources = [
        (vec_hbm.at[0], vec_ref), (nbr_hbm, nbr_ref), (type_hbm, type_ref),
        (count_hbm, count_ref), (flip_hbm, fliploc_ref), (basis_hbm.at[0], basis_ref),
        (hop_hbm, hop_ref), (soc_hbm, soc_ref), (pot_hbm, pot_ref)]
    loads = [
        pltpu.make_async_copy(src, dst, load_sem.at[n]) for n, (src, dst) in enumerate(sources)]
    for copy in loads:
        copy.start()
    groups = dom_total // group_doms
    group_size = 2 * group_doms
    dom, spin = lax.axis_index("dom"), lax.axis_index("spin")
    rank_a = (dom % group_doms) * 2 + spin
    rank_b = dom // group_doms
    dom_base = rank_b * group_doms
    left, right = (dom + dom_total - 1) % dom_total, (dom + 1) % dom_total

    def peer_a(shift):
        other = (rank_a + shift) % group_size
        return (dom_base + other // 2, other % 2)

    def peer_b(shift):
        return (((rank_b + shift) % groups) * group_doms + dom % group_doms, spin)

    far_first = sorted(range(dom_total), key=lambda shift: -min(shift, dom_total - shift))

    def everyone():
        for shift in far_first:
            ahead = dom + shift
            target = jnp.where(ahead >= dom_total, ahead - dom_total, ahead)
            if shift:
                yield (target, spin)
            yield (target, 1 - spin)

    barrier = pltpu.get_barrier_semaphore()
    if direct:
        greeted = list(everyone())
    else:
        greeted = [peer_a(shift) for shift in range(1, group_size)]
        greeted += [peer_b(shift) for shift in range(1, groups)]
        greeted += [(left, spin), (right, spin)]
    for target in greeted:
        pl.semaphore_signal(barrier, inc=1, device_id=target, device_id_type=MESH)

    lane = lax.broadcasted_iota(I32, (vecs, width), 1)
    row = lax.broadcasted_iota(I32, (vecs, width), 0)

    def cols(tile, size=1):
        return pl.ds(pl.multiple_of(tile * width, width), size * width)

    def flip_copy(app):
        return pltpu.make_async_remote_copy(
            src_ref=major_ref.at[app], dst_ref=other_ref.at[app],
            send_sem=flip_send.at[app], recv_sem=flip_recv.at[app],
            device_id=(dom, 1 - spin), device_id_type=MESH)

    def edge_copies(n, first, rows):
        part = pl.ds(first, rows)
        tail = pltpu.make_async_remote_copy(
            src_ref=split_ref.at[pl.ds(blocks - RANGE, RANGE), part],
            dst_ref=edge_ref.at[pl.ds(0, RANGE), part],
            send_sem=edge_send.at[n, 0], recv_sem=edge_recv.at[n, 0],
            device_id=(right, spin), device_id_type=MESH)
        head = pltpu.make_async_remote_copy(
            src_ref=split_ref.at[pl.ds(0, RANGE), part],
            dst_ref=edge_ref.at[pl.ds(RANGE, RANGE), part],
            send_sem=edge_send.at[n, 1], recv_sem=edge_recv.at[n, 1],
            device_id=(left, spin), device_id_type=MESH)
        return tail, head

    def to_major(value, scratch, base, store):
        for b, piece in enumerate(value):
            scratch[pl.ds(base + b * vecs, vecs), :] = piece
        for k in range(vecs):
            store(k, scratch[pl.ds(base + k, CHUNK, stride=vecs), :].astype(BF16))

    def tree(parts):
        while len(parts) > 1:
            parts = [sum(parts[p + 1:p + 2], parts[p]) for p in range(0, len(parts), 2)]
        return parts[0]

    def stage(n, ref, send, recv, rank, size, peer):
        def copy(shift, slot):
            return pltpu.make_async_remote_copy(
                src_ref=ref.at[n, rank], dst_ref=ref.at[n, slot],
                send_sem=send.at[n, shift], recv_sem=recv.at[n, slot],
                device_id=peer(shift), device_id_type=MESH)

        def begin(value):
            ref[n, rank] = value
            for shift in range(1, size):
                copy(shift, rank).start()

        def end():
            for shift in range(1, size):
                copy(shift, (rank + size - shift) % size).wait_recv()
            for shift in range(1, size):
                copy(shift, rank).wait_send()
            return tree([ref[n, slot] for slot in range(size)])
        return begin, end

    def staged(n):
        begin_a, end_a = stage(n, stage_a_ref, a_send, a_recv, rank_a, group_size, peer_a)
        begin_b, end_b = stage(n, stage_b_ref, b_send, b_recv, rank_b, groups, peer_b)
        return begin_a, lambda: begin_b(end_a()), end_b

    def exchange(n, ref):
        if not direct:
            return staged(n)
        me = dom * 2 + spin

        def begin(value):
            ref[me] = value
            for target in everyone():
                pltpu.make_async_remote_copy(
                    src_ref=ref.at[me], dst_ref=ref.at[me],
                    send_sem=all_send.at[n], recv_sem=all_recv.at[n],
                    device_id=target, device_id_type=MESH).start()

        def end():
            others = ref.at[pl.ds(0, devices - 1)]
            whole = pltpu.make_async_remote_copy(
                src_ref=others, dst_ref=others, send_sem=all_send.at[n], recv_sem=all_recv.at[n],
                device_id=(dom, 1 - spin), device_id_type=MESH)
            whole.wait_recv()
            whole.wait_send()
            return tree([ref[slot] for slot in range(devices)])
        return begin, lambda: None, end

    def share(n, ref, value, size, work):
        begin, middle, end = exchange(n, ref)
        if not direct:
            begin(value)
            done = work()
            middle()
            return end() * (1.0 / norm), done
        per = width // size
        rows = -(-vecs // per)
        out = value
        for q in range(1, per):
            moved = pltpu.roll(pltpu.roll(value, (-q * rows) % vecs, 0), q * size, 1)
            out = jnp.where((lane >= q * size) & (lane < (q + 1) * size), moved, out)
        begin(out[:rows])
        done = work()
        fold_ref[pl.ds(0, rows), :] = end()
        total = fold_ref[...] * (1.0 / norm)
        out = jnp.where((lane < size) & (row < rows), total, 0.0)
        for q in range(1, per):
            moved = pltpu.roll(pltpu.roll(total, (q * rows) % vecs, 0), width - q * size, 1)
            out = jnp.where((lane < size) & (row >= q * rows) & (row < (q + 1) * rows), moved, out)
        return out, done

    def lanes(value, start, size):
        moved = value if start == 0 else pltpu.roll(value, width - start, 1)
        return jnp.where(lane < size, moved, 0.0)

    def tall(pieces):
        pad = width - vecs * len(pieces)
        return jnp.concatenate(list(pieces) + [jnp.zeros((pad, width), F32)], axis=0)

    def folded(value):
        wide = value.shape[1]
        fold_ref[:, pl.ds(0, wide)] = value[:vecs] + value[vecs:]
        both = fold_ref[...]
        both = both + pltpu.roll(both, width - vecs, 1)
        out = jnp.where(lane < vecs, both, 0.0)
        for g in range(1, wide // pair):
            inside = (lane >= vecs * g) & (lane < vecs * (g + 1))
            out = jnp.where(inside, pltpu.roll(both, width - vecs * g, 1), out)
        return out

    def wide_rows(ref, first, rows, tiles):
        return jnp.concatenate([ref[tile, pl.ds(first, rows), :] for tile in tiles], axis=1)

    def gram(first, rows, size, tiles):
        tiles = list(tiles)
        step = max(len(tiles) // 4, 2)
        return tree([
            dot(wide_rows(split_ref, first, rows, part), wide_rows(split_ref, 0, size, part), NT)
            for part in (tiles[p:p + step] for p in range(0, len(tiles), step))])

    def prepare(span_gram, count):
        eye = jnp.where(wide_row == wide_lane, 1.0, 0.0)
        once = 2.0 * eye - span_gram
        left_over = high_dot(eye - span_gram, eye - span_gram, NN)
        square = once + high_dot(left_over, once, NN)
        for n, table in enumerate([once, square, left_over][:count]):
            high, low = halves(table)
            weight_ref[n, :, pl.ds(0, width)] = high
            weight_ref[n, :, pl.ds(width, width)] = low

    def factor(first_t, image_gram, span_count, count):
        first = split(first_t)
        mixed = []
        for n in range(count):
            out = dot(first, weight_ref[n], NN)
            out = out[:vecs] + out[vecs:]
            mixed.append(out[:, :width] + out[:, width:])
        total_t = mixed[0]
        out = dot(split(mixed[1]), first, NT)
        fold_ref[:, pl.ds(0, pair)] = out[:vecs] + out[vecs:]
        both = fold_ref[...]
        square = image_gram - both - pltpu.roll(both, width - vecs, 1)
        table = jnp.where(lane < vecs, square, jnp.where(lane == row + vecs, 1.0, 0.0))
        table = table - pltpu.roll(total_t, pair, 1)
        if count > 2:
            table = table + pltpu.roll(mixed[2], pair + span_count, 1)
        lower = jnp.zeros((vecs, width), F32)
        for j in range(vecs):
            column = jnp.broadcast_to(table[:, j:j + 1], (vecs, width))
            pivot_row = jnp.broadcast_to(table[j:j + 1, :], (vecs, width))
            pivot = jnp.broadcast_to(column[j:j + 1, :], (vecs, width))
            scale = lax.rsqrt(pivot)
            column = column * scale
            lower = jnp.where((lane == j) & (row >= j), column, lower)
            pivot_row = pivot_row * scale
            table = jnp.where(
                row == j, pivot_row, jnp.where(row > j, table - column * pivot_row, table))
        mixer = jnp.zeros((vecs, width), F32)
        for g in range(span_count // vecs + 1):
            source = pair + vecs * g if g < span_count // vecs else vecs
            moved = pltpu.roll(table, (pair * g - source) % width, 1)
            mixer = jnp.where((lane >= pair * g) & (lane < pair * g + vecs), moved, mixer)
        mixer = mixer + pltpu.roll(mixer, vecs, 1)
        low = mixer - mixer.astype(BF16).astype(F32)
        return (
            total_t + pltpu.roll(lower, span_count, 1), jnp.concatenate([mixer, low], axis=0), table)

    def split_products(out, k, base, half_size, size, ref):
        high, low = halves(out)
        ref[k, pl.ds(base, size), :] = high
        ref[k, pl.ds(half_size + base, size), :] = low

    def products(app):
        def body(two, carry):
            weights = hop_ref[pl.ds(pl.multiple_of(two * 2 * width, 2 * width), 2 * width), :]
            for k in range(vecs):
                out = dot(major_ref[app, k], weights, NT)
                for half in range(2):
                    at = pl.multiple_of((two * 2 + half) * blocks, blocks)
                    split_products(
                        out[:, half * width:(half + 1) * width], k, at, kinds * blocks, blocks,
                        prod_ref)
            return carry
        lax.fori_loop(0, types // 2, body, 0, unroll=2)

    def flip_products(app):
        for k in range(vecs):
            out = dot(other_ref[app, k], soc_ref[spin], NT)
            split_products(out, k, types * blocks, kinds * blocks, blocks, prod_ref)

    def gather():
        def body(two, carry):
            chosen = jnp.concatenate([select_ref[n % kinds] for n in range(2 * kinds)], axis=1)
            held = jnp.concatenate([prod_ref[2 * two], prod_ref[2 * two + 1]], axis=1)
            out = dot(chosen, held, NN)
            for half in range(2):
                for i in range(blocks // vecs):
                    block_ref[pl.ds(i * vecs * vecs + 2 * two + half, vecs, stride=vecs), :] = (
                        out[i * vecs:(i + 1) * vecs, half * width:(half + 1) * width])
            return carry
        lax.fori_loop(0, vecs // 2, body, 0, unroll=2)

    def edge_gather():
        reach = 2 * RANGE
        source = far_ref[...].reshape(vecs * reach, width)

        for two in range(types // 2):
            out = dot(source, hop_ref[pl.ds(two * 2 * width, 2 * width), :], NT)
            for half in range(2):
                for k in range(vecs):
                    split_products(
                        out[k * reach:(k + 1) * reach, half * width:(half + 1) * width], k,
                        (two * 2 + half) * reach, types * reach, reach, edge_prod_ref)
        chosen = jnp.concatenate([edge_select_ref[...]] * 2, axis=1)
        for two in range(vecs // 2):
            held = jnp.concatenate([edge_prod_ref[2 * two], edge_prod_ref[2 * two + 1]], axis=1)
            out = dot(chosen, held, NN)
            for half in range(2):
                for end, base in enumerate((0, (blocks - RANGE) * vecs)):
                    at = pl.ds(base + 2 * two + half, RANGE, stride=vecs)
                    block_ref[at, :] = block_ref[at, :] + out[
                        end * RANGE:(end + 1) * RANGE, half * width:(half + 1) * width]

    def assemble(field_ref, first, low, high):
        def body(block, carry):
            image = pot_ref[pl.ds(0, 1), cols(block)] * field_ref[:, cols(block)]
            at = pl.multiple_of(block * vecs, vecs)
            image = image + block_ref[pl.ds(at, vecs), :]
            split_ref[block, pl.ds(first, pair), :] = split(image)
            return carry
        lax.fori_loop(low, high, body, 0, unroll=16 if (high - low) % 16 == 0 else 8)

    def chunk_pieces(value):
        return [value[:, b * width:(b + 1) * width] for b in range(CHUNK)]

    def store_major(app, chunk):
        def store(k, rounded):
            major_ref[app, k, pl.ds(pl.multiple_of(chunk * CHUNK, CHUNK), CHUNK), :] = rounded
        return store

    def round_body(chunk, carry):
        pieces = chunk_pieces(vec_ref[:, cols(chunk * CHUNK, CHUNK)])
        for b, piece in enumerate(pieces):
            split_ref[chunk * CHUNK + b, pl.ds(2 * kept, pair), :] = split(piece)
        to_major(pieces, block_ref, chunk * CHUNK * vecs, store_major(0, chunk))
        return carry

    def store_far(k, rounded):
        far_ref[k] = rounded

    wide_row = lax.broadcasted_iota(I32, (width, width), 0)
    wide_lane = lax.broadcasted_iota(I32, (width, width), 1)
    chunks = blocks // CHUNK
    loads[0].wait()
    round_body(0, 0)
    round_body(chunks - 1, 0)
    pl.semaphore_wait(barrier, len(greeted))
    vec_edges = edge_copies(0, 2 * kept, pair)
    for copy in vec_edges:
        copy.start()
    lax.fori_loop(1, chunks - 1, round_body, 0)
    flip_one = flip_copy(0)
    flip_one.start()
    for copy in loads[1:5]:
        copy.wait()

    local = lax.broadcasted_iota(I32, (slots, blocks), 1)
    slot_at = lax.broadcasted_iota(I32, (slots, blocks), 0)
    shift = nbr_ref[...] - (dom * blocks + local) + RANGE
    total = dom_total * blocks
    shift = jnp.where(shift < 0, shift + total, shift)
    shift = jnp.where(shift >= total, shift - total, shift)
    place = local + shift - RANGE
    live = slot_at < count_ref[...]
    inside = (place >= 0) & (place < blocks)
    code = jnp.where(live & inside, type_ref[...] * STRIDE + shift, -1)
    edge_code = jnp.where(place < 0, place + RANGE, place - blocks + RANGE)
    edge_code = jnp.where(live & ~inside, type_ref[...] * (2 * RANGE) + edge_code, -1)

    def counts(codes, base):
        wanted = row + base
        return tree([jnp.where(codes[s:s + 1, :] == wanted, 1.0, 0.0) for s in range(slots)])

    band = (wide_lane - wide_row <= RANGE) & (wide_row - wide_lane <= RANGE)
    per_tile = width // STRIDE
    blank = jnp.zeros((vecs, width), F32)
    for tile in range(types // per_tile):
        pieces = []
        for r in range(width // vecs):
            live_rows = (r * vecs) % STRIDE <= 2 * RANGE
            pieces.append(counts(code, tile * width + r * vecs) if live_rows else blank)
        table = jnp.concatenate(pieces, axis=0).T
        for t in range(per_tile):
            moved = pltpu.roll(
                table, (-RANGE - STRIDE * t) % width, 1, stride=1, stride_axis=0)
            select_ref[tile * per_tile + t] = jnp.where(band, moved, 0.0).astype(BF16)
    flip_local = fliploc_ref[...] - dom * blocks
    select_ref[types] = jnp.where(flip_local == wide_row, 1.0, 0.0).T.astype(BF16)
    table = jnp.concatenate(
        [counts(edge_code, r * vecs) for r in range(width // vecs)], axis=0).T
    edge_select_ref[...] = jnp.concatenate(
        [table[:RANGE], table[blocks - RANGE:]], axis=0).astype(BF16)
    fold_ref[...] = jnp.zeros((vecs, width), F32)

    loads[5].wait()

    def split_basis(chunk, carry):
        for b in range(4):
            block = chunk * 4 + b
            for g in range(kept_groups):
                split_ref[block, pl.ds(g * pair, pair), :] = split(
                    basis_ref[pl.ds(g * vecs, vecs), cols(block)])
        return carry
    lax.fori_loop(0, blocks // 4, split_basis, 0, unroll=2)
    basis_edges = edge_copies(1, 0, 2 * kept)
    for copy in basis_edges:
        copy.start()
    low_gram = gram(0, rows_one, rows_one, range(blocks))
    packed_low = jnp.zeros((vecs, width), F32)
    for g in range(span_one // vecs):
        piece = folded(low_gram[g * pair:(g + 1) * pair])
        packed_low = packed_low + (pltpu.roll(piece, g * span_one, 1) if g else piece)
    low_begin, low_middle, low_end = exchange(0, all_low_ref)
    low_begin(packed_low)
    for copy in loads[6:]:
        copy.wait()

    products(0)
    low_middle()
    flip_one.wait_recv()
    flip_products(0)
    gather()
    assemble(vec_ref, rows_one, RANGE, blocks - RANGE)
    inner_ref[...] = gram(rows_one, pair, rows_two, range(RANGE, blocks - RANGE))
    for copy in vec_edges:
        copy.wait_recv()
    to_major(
        [edge_ref[b, pl.ds(2 * kept, pair), :].astype(F32)[:vecs] for b in range(2 * RANGE)],
        near_ref, 0, store_far)
    edge_gather()
    assemble(vec_ref, rows_one, 0, RANGE)
    assemble(vec_ref, rows_one, blocks - RANGE, blocks)
    image_edges = edge_copies(2, rows_one, pair)
    ends = list(range(RANGE)) + list(range(blocks - RANGE, blocks))
    result = folded(inner_ref[...] + gram(rows_one, pair, rows_two, ends))

    def while_sharing():
        for copy in image_edges:
            copy.start()
        packed = low_end() * (1.0 / norm)
        span_gram = tall(
            [lanes(packed, g * span_one, span_one) for g in range(span_one // vecs)])
        prepare(span_gram, 3)
        return span_gram
    packed, span_gram = share(1, all_one_ref, result, span_one + vecs, while_sharing)
    coefs, mixer, table = factor(
        lanes(packed, 0, span_one), lanes(packed, span_one, vecs), span_one, 3)
    small_ref[pl.ds(0, vecs), :] = coefs
    mixer = mixer.astype(BF16)[:, :rows_two]
    for copy in image_edges:
        copy.wait_send()

    def mix_body(chunk, carry):
        out = dot(
            mixer, wide_rows(split_ref, 0, rows_two, [chunk * CHUNK + b for b in range(CHUNK)]), NN)
        value = out[:vecs] + out[vecs:]
        one_ref[:, cols(chunk * CHUNK, CHUNK)] = value
        pieces = chunk_pieces(value)
        for b, piece in enumerate(pieces):
            split_ref[chunk * CHUNK + b, pl.ds(rows_one, pair), :] = split(piece)
        to_major(pieces, block_ref, chunk * CHUNK * vecs, store_major(1, chunk))
        return carry
    lax.fori_loop(0, chunks, mix_body, 0, unroll=2)
    flip_two = flip_copy(1)
    flip_two.start()
    products(1)
    for copy in image_edges + basis_edges:
        copy.wait_recv()
    out = dot(mixer, wide_rows(edge_ref, 0, rows_two, range(2 * RANGE)), NN)
    to_major(chunk_pieces(out[:vecs] + out[vecs:]), near_ref, 0, store_far)
    flip_two.wait_recv()
    flip_products(1)
    gather()
    edge_gather()
    assemble(one_ref, rows_two, 0, blocks)
    result = folded(gram(rows_two, pair, rows_two + pair, range(blocks)))

    def while_sharing_two():
        cross = lanes(table, pair + span_one, span_one)
        cross = cross + jnp.where(lane == row + span_one, 1.0, 0.0)
        low = jnp.concatenate(
            [jnp.zeros((span_one, width), F32), cross,
             jnp.zeros((width - span_two, width), F32)], axis=0)
        prepare(span_gram + low + jnp.where(
            (wide_row < span_one) & (wide_lane >= span_one), low.T, 0.0), 2)
        for copy in vec_edges + basis_edges:
            copy.wait_send()
        flip_one.wait_send()
        flip_two.wait_send()
    packed, _ = share(2, all_two_ref, result, span_two + vecs, while_sharing_two)
    coefs, mixer, _ = factor(
        lanes(packed, 0, span_two), lanes(packed, span_two, vecs), span_two, 2)
    small_ref[pl.ds(vecs, vecs), :] = coefs
    small_ref[pl.ds(pair, pair), :] = mixer


def finish(
    cfg, small_ref, split_ref, one_ref,
    one_hbm, two_hbm, coef_one_hbm, coef_two_hbm,
    two_ref, cut_one_ref, cut_two_ref, store_sem,
):
    _, _, blocks, width, _, _, vecs, kept, _, _ = cfg
    span_one = kept + vecs
    span_two = span_one + vecs
    pieces = 8
    size = blocks // pieces * width
    stores = [pltpu.make_async_copy(one_ref, one_hbm.at[0], store_sem.at[0])]
    stores[-1].start()
    mixer = small_ref[pl.ds(2 * vecs, 2 * vecs), :].astype(BF16)[:, :2 * (span_two + vecs)]
    for piece in range(pieces):
        part = pl.ds(piece * size, size)
        tiles = range(piece * (blocks // pieces), (piece + 1) * (blocks // pieces))
        out = dot(mixer, jnp.concatenate([split_ref[tile] for tile in tiles], axis=1), NN)
        two_ref[:, part] = out[:vecs] + out[vecs:]
        stores.append(pltpu.make_async_copy(
            two_ref.at[:, part], two_hbm.at[0, :, part], store_sem.at[1 + piece]))
        stores[-1].start()
    cut_one_ref[...] = small_ref[pl.ds(0, vecs), :span_one + vecs]
    cut_two_ref[...] = small_ref[pl.ds(vecs, vecs), :span_two + vecs]
    stores.append(pltpu.make_async_copy(cut_one_ref, coef_one_hbm, store_sem.at[1 + pieces]))
    stores.append(pltpu.make_async_copy(cut_two_ref, coef_two_hbm, store_sem.at[2 + pieces]))
    for copy in stores[-2:]:
        copy.start()
    for copy in stores:
        copy.wait()


def per_device(
    vectors, basis, potential, hop_table, soc_table, nbr_block, nbr_type, nbr_count, flip_block
):
    blocks, slots = nbr_block.shape
    types, width, _ = hop_table.shape
    vecs, kept = vectors.shape[1], basis.shape[1]
    dom_total = lax.axis_size("dom")
    group_doms = 4 if dom_total % 4 == 0 else 1
    groups = dom_total // group_doms
    norm = float(2 * blocks * width * dom_total)
    direct = dom_total <= 32
    cfg = (dom_total, group_doms, blocks, width, types, slots, vecs, kept, norm, direct)
    count = blocks * width
    pair = 2 * vecs
    span_one, span_two = kept + vecs, kept + 2 * vecs
    kinds = types + 1
    seats = 2 * dom_total if direct else 1
    rounds, near, far = (1, 1, 1) if direct else (3, 2 * group_doms, groups)
    row_count = lambda size: -(-vecs // (width // size))
    vmem = pl.BlockSpec(memory_space=pltpu.VMEM)
    hbm = pl.BlockSpec(memory_space=pltpu.HBM)
    dma = pltpu.SemaphoreType.DMA
    shape = jax.ShapeDtypeStruct
    one, parts, small = pl.pallas_call(
        functools.partial(kernel, cfg),
        name="krylov",
        out_shape=(
            pltpu.VMEM((vecs, count), F32),
            pltpu.VMEM((blocks, 2 * (span_two + vecs), width), BF16),
            pltpu.VMEM((4 * vecs, width), F32),
        ),
        in_specs=[hbm] * 9,
        out_specs=(vmem, vmem, vmem),
        scratch_shapes=[
            pltpu.VMEM((vecs, count), F32),
            pltpu.VMEM((kept, count), F32),
            pltpu.VMEM((1, count), F32),
            pltpu.VMEM((types * width, width), BF16),
            pltpu.VMEM(soc_table.shape, BF16),
            pltpu.VMEM((slots, blocks), I32),
            pltpu.VMEM((slots, blocks), I32),
            pltpu.VMEM((1, blocks), I32),
            pltpu.VMEM((1, blocks), I32),
            pltpu.VMEM((blocks * vecs, width), F32),
            pltpu.VMEM((2 * RANGE, 2 * span_two, width), BF16),
            pltpu.VMEM((2, vecs, blocks, width), BF16),
            pltpu.VMEM((2, vecs, blocks, width), BF16),
            pltpu.VMEM((2 * RANGE * vecs, width), F32),
            pltpu.VMEM((vecs, 2 * RANGE, width), BF16),
            pltpu.VMEM((vecs, 2 * kinds * blocks, width), BF16),
            pltpu.VMEM((vecs, 4 * RANGE * types, width), BF16),
            pltpu.VMEM((kinds, blocks, width), BF16),
            pltpu.VMEM((2 * RANGE, 2 * RANGE * types), BF16),
            pltpu.VMEM((vecs, width), F32),
            pltpu.VMEM((pair, 2 * span_two), F32),
            pltpu.VMEM((3, width, 2 * width), BF16),
            pltpu.VMEM((rounds, near, vecs, width), F32),
            pltpu.VMEM((rounds, far, vecs, width), F32),
            pltpu.VMEM((seats, vecs, width), F32),
            pltpu.VMEM((seats, row_count(span_one + vecs), width), F32),
            pltpu.VMEM((seats, row_count(span_two + vecs), width), F32),
            dma((9,)),
            dma((2,)), dma((2,)),
            dma((3, 2)), dma((3, 2)),
            dma((rounds, near)), dma((rounds, near)),
            dma((rounds, far)), dma((rounds, far)),
            dma((3,)), dma((3,)),
        ],
        compiler_params=pltpu.CompilerParams(
            collective_id=0, has_side_effects=True, vmem_limit_bytes=32 * 1024 * 1024),
    )(*[pltpu.with_memory_space_constraint(value, pltpu.HBM) for value in (
        vectors, basis, potential, hop_table.reshape(types * width, width), soc_table,
        nbr_block.T, nbr_type.T, nbr_count.reshape(1, blocks), flip_block.reshape(1, blocks))])
    one, two, coef_one, coef_two = pl.pallas_call(
        functools.partial(finish, cfg),
        name="finish",
        out_shape=(
            shape((1, vecs, count), F32),
            shape((1, vecs, count), F32),
            shape((vecs, span_one + vecs), F32),
            shape((vecs, span_two + vecs), F32),
        ),
        in_specs=[vmem, vmem, vmem],
        out_specs=(hbm,) * 4,
        scratch_shapes=[
            pltpu.VMEM((vecs, count), F32),
            pltpu.VMEM((vecs, span_one + vecs), F32),
            pltpu.VMEM((vecs, span_two + vecs), F32),
            dma((11,)),
        ],
        compiler_params=pltpu.CompilerParams(vmem_limit_bytes=16 * 1024 * 1024),
    )(small, parts, one)
    return one, two, coef_one.T, coef_two.T


def solution(mesh):
    return jax.shard_map(
        per_device,
        mesh=mesh,
        in_specs=(
            P("spin", None, "dom"),
            P("spin", None, "dom"),
            P("spin", "dom"),
            P(),
            P(),
            P("dom", None),
            P("dom", None),
            P("dom"),
            P("dom"),
        ),
        out_specs=(P("spin", None, "dom"), P("spin", None, "dom"), P(), P()),
        check_vma=False,
    )
```
